32 devices in a mesh: dp: 2 (over y), blk: 8 (over z, x), chan: 2 (over core).
Axes of the slice: x: 2, y: 2, z: 4, core: 2. Of those that a mesh axis runs over, the one named last changes fastest.
Arguments:
- features: bfloat16 [1024, 512], P(('dp', 'blk'), 'chan'), parts along dimension 0, may hold values from -6 to 6
- chrom_len: int32 [2], P('dp'), parts along dimension 0, may hold values from 320 to 512
- band_mask: int32 [16, 4], P('dp'), parts along dimension 0, may hold values 0 or 1
- conv_weight: bfloat16 [2, 3, 512, 512], P(None, None, None, 'chan'), may hold values from -0.15625 to 0.15625
- conv_bias: bfloat16 [2, 512], P(None, 'chan'), may hold values from -3 to 3
- proj_weight: bfloat16 [512, 128], replicated, may hold values from -0.25 to 0.25
- proj_bias: bfloat16 [128], replicated, may hold values from -3 to 3
- map_weight: bfloat16 [3, 3, 64, 64], P(None, None, 'chan'), may hold values from -0.25 to 0.25
- map_bias: bfloat16 [64], P('chan'), may hold values from -3 to 3
- head_weight: bfloat16 [64], P('chan'), may hold values from -0.75 to 0.75
Outputs:
- contact: float32 [1024, 256], P(('dp', 'blk'), 'chan'), parts along dimension 0
The draws below stay inside these ranges and needn't reach their ends.
There are 2 independent parts, one for each index of `dp`. The reference program is written for one: setup_inputs(seed, part) draws one part's arguments, and reference() takes and returns one part's arrays. A program takes and returns all parts, laid end to end along the dimension named above; an argument that names none is the same for every part. Nothing has to cross between parts.
Inputs may be any that keep to these rules, and one draw needn't show every extreme that they name: Bins from chrom_len[0] on are padding. `band_mask`: 1 marks a predicted tile.
All inputs are finite; a program needn't handle non-finite values.
Results may differ from the reference program's by a relative error of at most 0.0053.
Values may be sent and summed in bfloat16 or wider, within the bound.
A program may use at most 64 MiB of HBM per device.

```python
import jax
import jax.numpy as jnp
from jax import lax

C = 512
F2 = 64
BIN_DEV = 64
BAND = 3
CONV1 = 2
D2 = 2
NB = 512
N_BLK = 8


def set_ends(array, own_key, low, largest):
    extent = array.shape
    index_at = [jax.random.randint(jax.random.fold_in(own_key, axis), (), 0, extent[axis]) for axis in range(len(extent))]
    array = array.at[tuple(index_at)].set(low)
    longest = extent.index(max(extent))
    index_at[longest] = (index_at[longest] + 1) % extent[longest]
    return array.at[tuple(index_at)].set(largest)


def shard_levels(rng, shape, split, low, largest):
    loudness, own = 1.0, jax.random.fold_in(rng, 6)
    for dim, parts in split:
        draws = jnp.exp(jax.random.uniform(jax.random.fold_in(own, dim), (parts,), jnp.float32, low / len(split), largest / len(split)))
        loudness = loudness * jnp.repeat(draws, shape[dim] // parts).reshape([-1 if axis == dim else 1 for axis in range(len(shape))])
    return loudness


def noise(stream_key, extent, width, reach, cuts=(), kind=jnp.bfloat16):
    values = jax.random.normal(stream_key, extent, jnp.float32) * width
    if len(cuts) > 0:
        values = shard_levels(stream_key, extent, cuts, -0.22, 0.18) * values
    return jnp.clip(values, min=-reach, max=reach).astype(kind)


def setup_inputs(seed: int = 0, part: int = 0) -> dict:
    keys = jax.random.split(jax.random.key(seed), 11)
    part_keys = jax.random.split(jax.random.fold_in(keys[10], part), 11)
    return {
        "features": noise(part_keys[0], (NB, C), 1.0, 6.0, ((0, 8), (1, 2))),
        "chrom_len": jax.random.randint(part_keys[1], (1,), NB - 3 * BIN_DEV, NB + 1).astype(jnp.int32),
        "band_mask": set_ends((jax.random.randint(part_keys[2], (N_BLK, BAND + 1), 0, 4) < 3).astype(jnp.int32), jax.random.fold_in(part_keys[2], 1), 0, 1),
        "conv_weight": noise(keys[3], (CONV1, 3, C, C), (3 * C) ** -0.5, 0.15625, ((3, 2),)),
        "conv_bias": noise(keys[4], (CONV1, C), 0.5, 3.0, ((1, 2),)),
        "proj_weight": noise(keys[5], (C, 2 * F2), C ** -0.5, 0.25),
        "proj_bias": noise(keys[6], (2 * F2,), 0.5, 3.0),
        "map_weight": noise(keys[7], (3, 3, F2, F2), (9 * F2) ** -0.5, 0.25, ((2, 2),)),
        "map_bias": noise(keys[8], (F2,), 0.5, 3.0, ((0, 2),)),
        "head_weight": noise(keys[9], (F2,), F2 ** -0.5, 0.75, ((0, 2),)),
    }


def band_live(first_row, row_count, first_col, col_count, length, mask_table):
    row_bins = first_row + jnp.arange(row_count, dtype=jnp.int32)
    col_bins = first_col + jnp.arange(col_count, dtype=jnp.int32)
    row_blocks = jnp.floor_divide(row_bins, BIN_DEV)
    col_blocks = jnp.floor_divide(col_bins, BIN_DEV)
    offsets = col_blocks[None, :] - row_blocks[:, None]
    table_rows = jnp.take(mask_table, jnp.clip(row_blocks + 1, 0, N_BLK + 1), axis=0)
    result = jnp.zeros((row_count, col_count), jnp.float32)
    for offset_value in range(BAND + 1):
        result = result + jnp.where(offsets == offset_value, table_rows[:, offset_value:offset_value + 1], 0.0)
    row_valid = (row_bins >= 0) & (row_bins < length)
    col_valid = (col_bins >= 0) & (col_bins < length)
    return result * (row_valid[:, None] & col_valid[None, :]).astype(jnp.float32)


def reference(features, chrom_len, band_mask, conv_weight, conv_bias, proj_weight, proj_bias, map_weight, map_bias, head_weight):
    total_bins = features.shape[0]
    length = chrom_len[0]
    positions = jnp.arange(total_bins, dtype=jnp.int32)
    hidden_rows = jnp.where((positions < length)[:, None], features, jnp.zeros_like(features))
    for layer_index in range(CONV1):
        dilation = 2 ** (layer_index + 1)
        padded = jnp.pad(hidden_rows, ((dilation, dilation), (0, 0)))
        running = jnp.zeros((total_bins, C), jnp.float32)
        for tap_index in range(3):
            running = running + jnp.dot(padded[tap_index * dilation:tap_index * dilation + total_bins], conv_weight[layer_index, tap_index], preferred_element_type=jnp.float32)
        hidden_rows = (hidden_rows.astype(jnp.float32) + jax.nn.relu(running + conv_bias[layer_index].astype(jnp.float32))).astype(jnp.bfloat16)
    projected = (jnp.dot(hidden_rows, proj_weight, preferred_element_type=jnp.float32) + proj_bias.astype(jnp.float32)).astype(jnp.bfloat16)
    span_cols = (BAND + 1) * BIN_DEV
    row_proj = jnp.pad(projected[:, :F2].T, ((0, 0), (D2, D2)))
    col_proj = jnp.pad(projected[:, F2:].T, ((0, 0), (D2, span_cols + D2)))
    mask_table = jnp.pad(band_mask, ((1, 1), (0, 0))).astype(jnp.float32)
    weights_map = map_weight.astype(jnp.float32)
    bias_map = map_bias.astype(jnp.float32)[:, None, None]
    head_vector = head_weight.astype(jnp.float32)

    def strip_output(block_index):
        first_bin = block_index * BIN_DEV
        row_slab = lax.dynamic_slice_in_dim(row_proj, first_bin, BIN_DEV + 2 * D2, 1).astype(jnp.float32)
        col_slab = lax.dynamic_slice_in_dim(col_proj, first_bin, span_cols + 2 * D2, 1).astype(jnp.float32)
        live_area = band_live(first_bin - D2, BIN_DEV + 2 * D2, first_bin - D2, span_cols + 2 * D2, length, mask_table)
        pair_map = (jax.nn.relu(row_slab[:, :, None] + col_slab[:, None, :]) * live_area[None]).astype(jnp.bfloat16)
        pair_wide = pair_map.astype(jnp.float32)
        running = jnp.zeros((F2, BIN_DEV, span_cols), jnp.float32)
        for row_tap in range(3):
            for col_tap in range(3):
                window = pair_wide[:, row_tap * D2:row_tap * D2 + BIN_DEV, col_tap * D2:col_tap * D2 + span_cols]
                running = running + jnp.einsum('ok,kab->oab', weights_map[row_tap, col_tap], window, precision=lax.Precision.HIGHEST)
        centre = pair_wide[:, D2:D2 + BIN_DEV, D2:D2 + span_cols]
        mixed = centre + jax.nn.relu(running + bias_map)
        contact = jnp.einsum('o,oab->ab', head_vector, mixed, precision=lax.Precision.HIGHEST)
        return contact * live_area[D2:D2 + BIN_DEV, D2:D2 + span_cols]

    strips = lax.map(strip_output, jnp.arange(N_BLK, dtype=jnp.int32))
    return strips.reshape(total_bins, span_cols)
```

```python
import jax
import jax.numpy as jnp
from jax import lax
from jax.experimental import pallas as pl
from jax.experimental.pallas import tpu as pltpu
from jax.sharding import PartitionSpec as P

F2 = 64
BAND = 3
D2 = 2
NEG = float("-inf")
HALO = 8
RIM = 16
TILE_STEP = 4
SLOT = (1, 2, 0, 3)
NT = (((1,), (1,)), ((), ()))


def copy_plan(bins):
    return [
        (0, None, 0, bins),
        (-1, 0, bins - RIM, RIM),
        (-1, 1, bins - RIM, RIM),
        (1, 0, 0, bins),
        (1, 1, 0, RIM),
        (1, 1, bins - RIM, RIM),
        (2, 1, 0, bins),
        (2, 0, 0, RIM),
        (3, 1, 0, bins),
        (4, 1, 0, RIM),
    ]


def kernel(
    n_blk,
    bins,
    len_ref,
    mask_hbm,
    x_hbm,
    cw_hbm,
    cb_hbm,
    pw_hbm,
    pb_hbm,
    mw_hbm,
    mb_hbm,
    hw_hbm,
    out_ref,
    feat,
    wts,
    cbias,
    pwt,
    pbias,
    mwt,
    mbias,
    head,
    mapt,
    mapw,
    pw4,
    pa_ref,
    pb_ref,
    pb4_ref,
    q_ref,
    gate_ref,
    mask_ref,
    wide_ref,
    pbn_ref,
    send_sem,
    recv_sem,
    psend_sem,
    precv_sem,
    loc_sem,
):
    dp = lax.axis_index("dp")
    blk = lax.axis_index("blk")
    chan = lax.axis_index("chan")
    other = 1 - chan
    half = x_hbm.shape[1]
    plan = copy_plan(bins)

    def dev(b, c):
        return (dp, b, c)

    barrier = pltpu.get_barrier_semaphore()

    def signal(b, c):
        pl.semaphore_signal(
            barrier, inc=1, device_id=dev(b, c), device_id_type=pl.DeviceIdType.MESH
        )

    signal(blk, other)
    for d in (-1, 1, 2, 3, 4):
        inside = (blk + d >= 0) & (blk + d < n_blk)
        if d >= 3:
            inside = inside & (chan == 1)

        @pl.when(inside)
        def _(d=d):
            signal(blk + d, 0)
            signal(blk + d, 1)

    locals_ = [
        pltpu.make_async_copy(x_hbm, feat.at[chan, pl.ds(RIM, bins)], loc_sem.at[0]),
        pltpu.make_async_copy(mw_hbm, mwt.at[chan], loc_sem.at[1]),
        pltpu.make_async_copy(mb_hbm, mbias.at[chan], loc_sem.at[2]),
        pltpu.make_async_copy(hw_hbm, head.at[chan], loc_sem.at[3]),
        pltpu.make_async_copy(cb_hbm, cbias.at[chan], loc_sem.at[4]),
        pltpu.make_async_copy(cw_hbm.at[0], wts.at[chan, 0], loc_sem.at[5]),
        pltpu.make_async_copy(cw_hbm.at[1], wts.at[chan, 1], loc_sem.at[6]),
        pltpu.make_async_copy(pw_hbm, pwt, loc_sem.at[7]),
        pltpu.make_async_copy(pb_hbm, pbias, loc_sem.at[8]),
        pltpu.make_async_copy(mask_hbm, mask_ref, loc_sem.at[9]),
    ]
    for copy in locals_:
        copy.start()

    def has(d):
        return jnp.where((blk - d >= 0) & (blk - d < n_blk), 1, 0)

    pl.semaphore_wait(barrier, 1 + 2 * has(-1) + 2 * has(1) + 2 * has(2) + has(3) + has(4))

    def feature_copy(index, sender_chan):
        d, rc, row, count = plan[index]
        return pltpu.make_async_remote_copy(
            src_ref=x_hbm.at[pl.ds(row, count)],
            dst_ref=feat.at[sender_chan, pl.ds(RIM + d * bins + row, count)],
            send_sem=send_sem.at[index],
            recv_sem=recv_sem.at[index, sender_chan],
            device_id=dev(blk - d, other if rc is None else rc),
            device_id_type=pl.DeviceIdType.MESH,
        )

    def partner_copy(slot, src, dst):
        return pltpu.make_async_remote_copy(
            src_ref=src,
            dst_ref=dst,
            send_sem=psend_sem.at[slot],
            recv_sem=precv_sem.at[slot],
            device_id=dev(blk, other),
            device_id_type=pl.DeviceIdType.MESH,
        )

    for index in (9, 8, 7, 6, 1, 2, 4, 5, 3):
        d = plan[index][0]

        @pl.when((blk - d >= 0) & (blk - d < n_blk))
        def _(index=index):
            feature_copy(index, chan).start()

    def partner_list(c):
        return [
            (mw_hbm, mwt.at[c]),
            (mb_hbm, mbias.at[c]),
            (hw_hbm, head.at[c]),
            (cb_hbm, cbias.at[c]),
            (cw_hbm.at[0], wts.at[c, 0]),
            (cw_hbm.at[1], wts.at[c, 1]),
        ]

    out_list = partner_list(chan)
    in_list = partner_list(other)

    def start_partner(slot):
        partner_copy(slot, *out_list[slot]).start()

    def wait_partner(slot):
        partner_copy(slot, *in_list[slot]).wait_recv()

    for slot in (0, 1, 2, 3):
        start_partner(slot)
    feature_copy(0, chan).start()
    start_partner(4)
    start_partner(5)

    mapt[...] = jnp.zeros_like(mapt)
    for slot in (1, 2, 3):
        locals_[slot].wait()
    for slot in (0, 1, 2):
        wait_partner(slot)
    ho = mw_hbm.shape[2]
    for side in range(2):
        for s in range(3):
            for t in range(3):
                block = mwt[side, s, t]
                for k1 in range(2):
                    for k2 in range(2):
                        r0 = (2 * k2 + k1) * F2 + side * ho
                        c0 = (s + k1) * 256 + SLOT.index(t + k2) * F2
                        mapt[r0 : r0 + ho, c0 : c0 + F2] = block
    mapw[...] = jnp.transpose(mapt[...])
    locals_[7].wait()
    locals_[8].wait()
    for part in range(2):
        block = pwt[:, part * F2 : (part + 1) * F2]
        for twice in range(2):
            at = (2 * part + twice) * F2
            pw4[:, at : at + F2] = block
    proj_b = pbias[...].astype(jnp.float32)
    proj_b = jnp.concatenate(
        [proj_b[:, :F2], proj_b[:, :F2], proj_b[:, F2:], proj_b[:, F2:]], axis=1
    )
    sel_row = lax.broadcasted_iota(jnp.int32, (ho, 512), 0)
    sel_lane = lax.broadcasted_iota(jnp.int32, (ho, 512), 1) % F2
    bias_row = jnp.zeros((1, 512), jnp.float32)
    head_row = jnp.zeros((1, 512), jnp.float32)
    for side in range(2):
        spread = jnp.where(sel_lane == sel_row + side * ho, 1.0, 0.0).astype(jnp.bfloat16)
        bias_row += jnp.dot(mbias[side], spread, preferred_element_type=jnp.float32)
        head_row += jnp.dot(head[side], spread, preferred_element_type=jnp.float32)
    bias_map = bias_row[:, :128]
    h_row = lax.broadcasted_iota(jnp.int32, (8, 512), 0)
    h_lane = lax.broadcasted_iota(jnp.int32, (8, 512), 1) // F2
    h_want = (h_lane // 4) * 4 + (h_lane // 2) % 2 + 2 * (h_lane % 2)
    head_mat = jnp.where(
        h_row == h_want, jnp.broadcast_to(head_row, (8, 512)), 0.0
    ).astype(jnp.bfloat16)
    locals_[9].wait()

    seg_a = bins + 2 * HALO
    seg_b = 2 * bins + 2 * HALO
    rows = seg_a + seg_b
    sub_b = lax.broadcasted_iota(jnp.int32, (seg_b, 128), 0)
    col_block = (chan * 2 * bins - HALO + bins + sub_b) // bins - 1

    def live_cols(block_shift, col_blk):
        at = blk + block_shift
        inside = (at >= 0) & (at < n_blk)
        at = lax.rem(at + n_blk, n_blk)
        live = jnp.zeros(col_blk.shape, jnp.int32)
        for o in range(BAND + 1):
            flag = jnp.where(inside, mask_ref[o, at], 0)
            live = jnp.where(col_blk - block_shift == o, flag, live)
        return live

    for v in range(3):
        gate_ref[v] = jnp.where(live_cols(v - 1, col_block) > 0, 0.0, NEG)

    feature_len = len_ref[0]
    total = n_blk * bins
    locals_[0].wait()
    locals_[4].wait()
    locals_[5].wait()
    feature_copy(0, other).wait_recv()
    for index, (d, rc, row, count) in enumerate(plan):
        if rc is None:
            continue

        @pl.when((blk + d >= 0) & (blk + d < n_blk) & (chan == rc))
        def _(index=index):
            feature_copy(index, 0).wait_recv()
            feature_copy(index, 1).wait_recv()

    wait_partner(3)
    wait_partner(4)

    start_b = pl.multiple_of(chan * 2 * bins, 2 * bins)
    skip = RIM - HALO
    sides = []
    for side in range(2):
        part_a = feat[side, 0 : bins + 2 * RIM].astype(jnp.float32)
        part_b = feat[side, pl.ds(start_b, 2 * bins + 2 * RIM)].astype(jnp.float32)
        sides.append(
            jnp.concatenate([part_a[skip : skip + seg_a], part_b[skip : skip + seg_b]], axis=0)
        )
    x = jnp.concatenate(sides, axis=1)

    def bin_of(shape):
        r = lax.broadcasted_iota(jnp.int32, shape, 0)
        return blk * bins - HALO + r + jnp.where(r < seg_a, 0, chan * 2 * bins - seg_a)

    bin_p = bin_of((rows, 128))
    ok_p = (bin_p >= 0) & (bin_p < feature_len)
    in_p = (bin_p >= 0) & (bin_p < total)

    def keep(mask, value):
        return jnp.concatenate(
            [
                jnp.where(mask, value[:, at : at + 128], 0.0)
                for at in range(0, value.shape[1], 128)
            ],
            axis=1,
        )

    x = keep(ok_p, x)

    def layer(h, level):
        e = 2 ** (level + 1)
        taps = [
            pltpu.roll(h, e, 0).astype(jnp.bfloat16),
            h.astype(jnp.bfloat16),
            pltpu.roll(h, rows - e, 0).astype(jnp.bfloat16),
        ]
        parts = []
        for side in range(2):
            acc = jnp.dot(taps[0], wts[side, level, 0], preferred_element_type=jnp.float32)
            for t in (1, 2):
                acc += jnp.dot(taps[t], wts[side, level, t], preferred_element_type=jnp.float32)
            bias = cbias[side, level : level + 1].astype(jnp.float32)
            parts.append(jax.nn.relu(acc + bias))
        return (h + jnp.concatenate(parts, axis=1)).astype(jnp.bfloat16).astype(jnp.float32)

    h = layer(x, 0)
    h = keep(in_p, h)
    locals_[6].wait()
    wait_partner(5)
    h = layer(h, 1)
    proj = (
        (jnp.dot(h.astype(jnp.bfloat16), pw4[...], preferred_element_type=jnp.float32) + proj_b)
        .astype(jnp.bfloat16)
        .astype(jnp.float32)
    )
    pa_ref[...] = jnp.where(ok_p[:seg_a], proj[:seg_a, :128], NEG)
    pb = jnp.where(ok_p[seg_a:], proj[seg_a:, 128:], NEG)
    for v in range(3):
        pb_ref[v] = pb + gate_ref[v]

    cols = 2 * bins
    n_tile = cols // 64
    low_lane = lax.broadcasted_iota(jnp.int32, (16, 128), 1) < F2
    for v in range(3):
        for t in range(n_tile):
            for p in range(2):
                taps = [
                    pb_ref[v, pl.ds(HALO + 64 * t + p + (SLOT[k] - 1) * D2, 16, stride=4), :]
                    for k in range(4)
                ]
                for k in range(2):
                    both = jnp.where(low_lane, taps[2 * k], taps[2 * k + 1])
                    pb4_ref[v, t, 16 * p : 16 * p + 16, 128 * k : 128 * k + 128] = both.astype(
                        jnp.bfloat16
                    )

    def build(r, t):
        v = 0 if r < D2 else (2 if r >= bins + D2 else 1)
        at = r + HALO - D2
        row = jnp.broadcast_to(pa_ref[at : at + 1, :], (16, 128)).astype(jnp.bfloat16)
        row = jnp.concatenate([jnp.concatenate([row, row], axis=1)] * 2, axis=0)
        q_ref[r, t] = jnp.maximum(pb4_ref[v, t] + row, jnp.bfloat16(0))

    out_row = lax.broadcasted_iota(jnp.int32, (8, cols), 0)
    out_lane = lax.broadcasted_iota(jnp.int32, (8, cols), 1) + chan * cols
    live_row = live_cols(0, out_lane // bins)
    live_row = jnp.where(blk * bins + out_lane < feature_len, live_row, 0)

    pbn_ref[...] = pb_ref[1, HALO : HALO + cols, :].astype(jnp.bfloat16)
    low_row = lax.broadcasted_iota(jnp.int32, (1, 128), 1) < F2
    bases = (0, 1, 4, 5)

    def conv(first):
        windows = jnp.concatenate(
            [
                jnp.concatenate([q_ref[8 * g + a + 2 * j, t] for j in range(4)], axis=1)
                for g in range(first, first + TILE_STEP)
                for t in range(n_tile)
                for a in bases
            ],
            axis=0,
        )
        wide = jnp.dot(windows, mapw[...], preferred_element_type=jnp.float32)
        at = 0
        for g in range(first, first + TILE_STEP):
            for t in range(n_tile):
                for j in range(4):
                    for p in range(2):
                        for k in range(2):
                            wide_ref[4 * g + j, pl.ds(64 * t + p + 2 * k, 16, stride=4), :] = wide[
                                at : at + 16, 128 * k : 128 * k + 128
                            ]
                        at += 16

    def finish(first):
        for g in range(first, first + TILE_STEP):
            sides = []
            for j, a in enumerate(bases):
                acc = jax.nn.relu(wide_ref[4 * g + j] + bias_map).astype(jnp.bfloat16)
                at = 8 * g + a + HALO
                row = jnp.where(low_row, pa_ref[at : at + 1, :], pa_ref[at + D2 : at + D2 + 1, :])
                row = jnp.broadcast_to(row, (16, 128)).astype(jnp.bfloat16)
                row = jnp.concatenate([row] * (cols // 16), axis=0)
                sides.append(acc + jnp.maximum(pbn_ref[...] + row, jnp.bfloat16(0)))
            mixed = jnp.concatenate(sides, axis=1)
            result = lax.dot_general(head_mat, mixed, NT, preferred_element_type=jnp.float32)
            live = jnp.where(blk * bins + 8 * g + out_row < feature_len, live_row, 0)
            out_ref[8 * g : 8 * g + 8, :] = jnp.where(live > 0, result, 0.0)

    done = 0
    for first in range(0, bins // 8, TILE_STEP):
        upto = 8 * (first + TILE_STEP) + 2 * D2
        for r in range(done, upto):
            for t in range(n_tile):
                build(r, t)
        done = upto
        conv(first)
        if first > 0:
            finish(first - TILE_STEP)
    finish(bins // 8 - TILE_STEP)

    for slot in range(6):
        partner_copy(slot, *out_list[slot]).wait_send()
    for index in range(len(plan)):
        d = plan[index][0]

        @pl.when((blk - d >= 0) & (blk - d < n_blk))
        def _(index=index):
            feature_copy(index, chan).wait_send()


def local(
    features,
    chrom_len,
    band_mask,
    conv_weight,
    conv_bias,
    proj_weight,
    proj_bias,
    map_weight,
    map_bias,
    head_weight,
):
    import functools

    bins, half = features.shape
    n_blk = lax.axis_size("blk")
    bf = jnp.bfloat16
    any_spec = pl.BlockSpec(memory_space=pltpu.HBM)
    smem = pl.BlockSpec(memory_space=pltpu.SMEM)
    rows = 4 * bins + 2 * RIM
    ho = map_weight.shape[2]
    return pl.pallas_call(
        functools.partial(kernel, n_blk, bins),
        out_shape=pltpu.VMEM((bins, 2 * bins), jnp.float32),
        in_specs=[smem] + [any_spec] * 9,
        out_specs=pl.BlockSpec(memory_space=pltpu.VMEM),
        scratch_shapes=[
            pltpu.VMEM((2, rows, half), bf),
            pltpu.VMEM((2,) + conv_weight.shape, bf),
            pltpu.VMEM((2,) + conv_bias.shape, bf),
            pltpu.VMEM(proj_weight.shape, bf),
            pltpu.VMEM((1, 2 * F2), bf),
            pltpu.VMEM((2,) + map_weight.shape, bf),
            pltpu.VMEM((2, 1, ho), bf),
            pltpu.VMEM((2, 1, ho), bf),
            pltpu.VMEM((256, 1024), bf),
            pltpu.VMEM((1024, 256), bf),
            pltpu.VMEM((proj_weight.shape[0], 256), bf),
            pltpu.VMEM((bins + 2 * HALO, 128), jnp.float32),
            pltpu.VMEM((3, 2 * bins + 2 * HALO, 128), jnp.float32),
            pltpu.VMEM((3, 2, 32, 256), bf),
            pltpu.VMEM((bins + 2 * D2, 2, 32, 256), bf),
            pltpu.VMEM((3, 2 * bins + 2 * HALO, 128), jnp.float32),
            pltpu.SMEM((BAND + 1, n_blk), jnp.int32),
            pltpu.VMEM((bins // 2, 2 * bins, 128), jnp.float32),
            pltpu.VMEM((2 * bins, 128), bf),
            pltpu.SemaphoreType.DMA((10,)),
            pltpu.SemaphoreType.DMA((10, 2)),
            pltpu.SemaphoreType.DMA((6,)),
            pltpu.SemaphoreType.DMA((6,)),
            pltpu.SemaphoreType.DMA((10,)),
        ],
        compiler_params=pltpu.CompilerParams(
            collective_id=0, has_side_effects=True, vmem_limit_bytes=60 * 2**20
        ),
        name="contact",
    )(
        chrom_len,
        band_mask.T,
        features,
        conv_weight,
        conv_bias,
        proj_weight,
        proj_bias.reshape(1, -1),
        map_weight,
        map_bias.reshape(1, -1),
        head_weight.reshape(1, -1),
    )


def solution(mesh):
    return jax.shard_map(
        local,
        mesh=mesh,
        in_specs=(
            P(("dp", "blk"), "chan"),
            P("dp"),
            P("dp", None),
            P(None, None, None, "chan"),
            P(None, "chan"),
            P(),
            P(),
            P(None, None, "chan", None),
            P("chan"),
            P("chan"),
        ),
        out_specs=P(("dp", "blk"), "chan"),
        check_vma=False,
    )
```

```python
import jax
import jax.numpy as jnp
from jax import lax
from jax.experimental import pallas as pl
from jax.experimental.pallas import tpu as pltpu
from jax.sharding import PartitionSpec as P

F2 = 64
BAND = 3
D2 = 2
NEG = float("-inf")
HALO = 8
TILE_STEP = 4
SLOT = (1, 2, 0, 3)
NT = (((1,), (1,)), ((), ()))


PLAN = {
    -1: ((0, "last", 0), (1, "last", 0)),
    1: ((1, "both", 1), (0, "first", 1), (0, "full", 2)),
    2: ((1, "full", 1), (0, "first", 3)),
    3: ((1, "full", 2),),
    4: ((1, "first", 3),),
}
ORDER = (4,3,2,-1,1)
INDEX = {(d, n): k for k, (d, n) in enumerate((d, n) for d in PLAN for n in range(len(PLAN[d])))}


def kernel(
    n_blk,
    bins,
    len_ref,
    mask_hbm,
    x_hbm,
    cw_hbm,
    cb_hbm,
    pw_hbm,
    pb_hbm,
    mw_hbm,
    mb_hbm,
    hw_hbm,
    out_ref,
    feat,
    rim_out,
    rim_in,
    wts,
    cbias,
    pwt,
    pbias,
    mwt,
    mbias,
    head,
    mapt,
    mapw,
    pw4,
    pa_ref,
    pb_ref,
    pb4_ref,
    q_ref,
    gate_ref,
    mask_ref,
    wide_ref,
    pbn_ref,
    send_sem,
    recv_sem,
    psend_sem,
    precv_sem,
    loc_sem,
):
    dp = lax.axis_index("dp")
    blk = lax.axis_index("blk")
    chan = lax.axis_index("chan")
    other = 1 - chan
    half = x_hbm.shape[1]

    def dev(b, c):
        return (dp, b, c)

    barrier = pltpu.get_barrier_semaphore()

    def signal(b, c):
        pl.semaphore_signal(
            barrier, inc=1, device_id=dev(b, c), device_id_type=pl.DeviceIdType.MESH
        )

    signal(blk, other)
    for d in (-1, 1, 2, 3, 4):
        inside = (blk + d >= 0) & (blk + d < n_blk)
        if d >= 3:
            inside = inside & (chan == 1)

        @pl.when(inside)
        def _(d=d):
            signal(blk + d, 0)
            signal(blk + d, 1)

    locals_ = [
        pltpu.make_async_copy(x_hbm, feat.at[chan, 0], loc_sem.at[0]),
        pltpu.make_async_copy(mw_hbm, mwt.at[chan], loc_sem.at[1]),
        pltpu.make_async_copy(mb_hbm, mbias.at[chan], loc_sem.at[2]),
        pltpu.make_async_copy(hw_hbm, head.at[chan], loc_sem.at[3]),
        pltpu.make_async_copy(cb_hbm, cbias.at[chan], loc_sem.at[4]),
        pltpu.make_async_copy(cw_hbm.at[0], wts.at[chan, 0], loc_sem.at[5]),
        pltpu.make_async_copy(cw_hbm.at[1], wts.at[chan, 1], loc_sem.at[6]),
        pltpu.make_async_copy(pw_hbm, pwt, loc_sem.at[7]),
        pltpu.make_async_copy(pb_hbm, pbias, loc_sem.at[8]),
        pltpu.make_async_copy(mask_hbm, mask_ref, loc_sem.at[9]),
    ]
    for copy in locals_:
        copy.start()

    locals_[0].wait()
    for side in range(2):
        edge = feat[chan, 0, 0:16] if side == 0 else feat[chan, 0, bins - 16 : bins]
        edge = edge.astype(jnp.float32)[8 * side : 8 * side + 8]
        rim_out[side] = jnp.concatenate([edge[:, :128], edge[:, 128:]], axis=0).astype(
            jnp.bfloat16
        )

    def has(d):
        return jnp.where((blk - d >= 0) & (blk - d < n_blk), 1, 0)

    pl.semaphore_wait(barrier, 1 + 2 * has(-1) + 2 * has(1) + 2 * has(2) + has(3) + has(4))

    def feature_copy(d, n, sender):
        rc, kind, slot = PLAN[d][n]
        if kind == "full":
            src, dst = feat.at[sender, 0], feat.at[sender, slot]
        elif kind == "both":
            src, dst = rim_out, rim_in.at[sender, pl.ds(slot, 2)]
        else:
            src, dst = rim_out.at[0 if kind == "first" else 1], rim_in.at[sender, slot]
        return pltpu.make_async_remote_copy(
            src_ref=src,
            dst_ref=dst,
            send_sem=send_sem.at[INDEX[d, n]],
            recv_sem=recv_sem.at[INDEX[d, n], sender],
            device_id=dev(blk - d, rc),
            device_id_type=pl.DeviceIdType.MESH,
        )

    def partner_copy(slot, src, dst):
        return pltpu.make_async_remote_copy(
            src_ref=src,
            dst_ref=dst,
            send_sem=psend_sem.at[slot],
            recv_sem=precv_sem.at[slot],
            device_id=dev(blk, other),
            device_id_type=pl.DeviceIdType.MESH,
        )

    for d in ORDER:

        @pl.when((blk - d >= 0) & (blk - d < n_blk))
        def _(d=d):
            for n in range(len(PLAN[d])):
                feature_copy(d, n, chan).start()

    def partner_list(c):
        return [
            (mw_hbm, mwt.at[c]),
            (mb_hbm, mbias.at[c]),
            (hw_hbm, head.at[c]),
            (cb_hbm, cbias.at[c]),
            (cw_hbm.at[0], wts.at[c, 0]),
            (cw_hbm.at[1], wts.at[c, 1]),
            (x_hbm, feat.at[c, 0]),
        ]

    out_list = partner_list(chan)
    in_list = partner_list(other)

    def start_partner(slot):
        partner_copy(slot, *out_list[slot]).start()

    def wait_partner(slot):
        partner_copy(slot, *in_list[slot]).wait_recv()

    for slot in (0, 1, 2, 3, 6):
        start_partner(slot)
    start_partner(4)
    start_partner(5)

    mapt[...] = jnp.zeros_like(mapt)
    for slot in (1, 2, 3):
        locals_[slot].wait()
    for slot in (0, 1, 2):
        wait_partner(slot)
    ho = mw_hbm.shape[2]
    for side in range(2):
        for s in range(3):
            for t in range(3):
                block = mwt[side, s, t]
                for k1 in range(2):
                    for k2 in range(2):
                        r0 = (2 * k2 + k1) * F2 + side * ho
                        c0 = (s + k1) * 256 + SLOT.index(t + k2) * F2
                        mapt[r0 : r0 + ho, c0 : c0 + F2] = block
    mapw[...] = jnp.transpose(mapt[...])
    locals_[7].wait()
    locals_[8].wait()
    for part in range(2):
        block = pwt[:, part * F2 : (part + 1) * F2]
        for twice in range(2):
            at = (2 * part + twice) * F2
            pw4[:, at : at + F2] = block
    proj_b = pbias[...].astype(jnp.float32)
    proj_b = jnp.concatenate(
        [proj_b[:, :F2], proj_b[:, :F2], proj_b[:, F2:], proj_b[:, F2:]], axis=1
    )
    sel_row = lax.broadcasted_iota(jnp.int32, (ho, 512), 0)
    sel_lane = lax.broadcasted_iota(jnp.int32, (ho, 512), 1) % F2
    bias_row = jnp.zeros((1, 512), jnp.float32)
    head_row = jnp.zeros((1, 512), jnp.float32)
    for side in range(2):
        spread = jnp.where(sel_lane == sel_row + side * ho, 1.0, 0.0).astype(jnp.bfloat16)
        bias_row += jnp.dot(mbias[side], spread, preferred_element_type=jnp.float32)
        head_row += jnp.dot(head[side], spread, preferred_element_type=jnp.float32)
    bias_map = bias_row[:, :128]
    h_row = lax.broadcasted_iota(jnp.int32, (8, 512), 0)
    h_lane = lax.broadcasted_iota(jnp.int32, (8, 512), 1) // F2
    h_want = (h_lane // 4) * 4 + (h_lane // 2) % 2 + 2 * (h_lane % 2)
    head_mat = jnp.where(
        h_row == h_want, jnp.broadcast_to(head_row, (8, 512)), 0.0
    ).astype(jnp.bfloat16)
    locals_[9].wait()

    seg_a = bins + 2 * HALO
    seg_b = 2 * bins + 2 * HALO
    rows = seg_a + seg_b
    sub_b = lax.broadcasted_iota(jnp.int32, (seg_b, 128), 0)
    col_block = (chan * 2 * bins - HALO + bins + sub_b) // bins - 1

    def live_cols(block_shift, col_blk):
        at = blk + block_shift
        inside = (at >= 0) & (at < n_blk)
        at = lax.rem(at + n_blk, n_blk)
        live = jnp.zeros(col_blk.shape, jnp.int32)
        for o in range(BAND + 1):
            flag = jnp.where(inside, mask_ref[o, at], 0)
            live = jnp.where(col_blk - block_shift == o, flag, live)
        return live

    for v in range(3):
        gate_ref[v] = jnp.where(live_cols(v - 1, col_block) > 0, 0.0, NEG)

    feature_len = len_ref[0]
    total = n_blk * bins
    locals_[4].wait()
    locals_[5].wait()
    for slot in range(7):
        partner_copy(slot, *out_list[slot]).wait_send()
    for d in PLAN:

        @pl.when((blk - d >= 0) & (blk - d < n_blk))
        def _(d=d):
            for n in range(len(PLAN[d])):
                feature_copy(d, n, chan).wait_send()

    wait_partner(6)
    for d in PLAN:
        for rc in range(2):
            mine = [n for n, entry in enumerate(PLAN[d]) if entry[0] == rc]
            if not mine:
                continue

            @pl.when((blk + d >= 0) & (blk + d < n_blk) & (chan == rc))
            def _(d=d, mine=mine):
                for n in mine:
                    feature_copy(d, n, 0).wait_recv()
                    feature_copy(d, n, 1).wait_recv()

    wait_partner(3)
    wait_partner(4)

    left = jnp.where(chan == 0, 0, 2)
    near = jnp.where(chan == 0, 0, 1)
    sides = []
    for side in range(2):
        edges = [rim_in[side, k].astype(jnp.float32) for k in (0, 1, left, 3)]
        edges = [jnp.concatenate([edge[:8], edge[8:]], axis=1) for edge in edges]
        block = [feat[side, k].astype(jnp.float32) for k in (0, near, 2)]
        sides.append(
            jnp.concatenate(
                [edges[0], block[0], edges[1], edges[2], block[1], block[2], edges[3]], axis=0
            )
        )
    x = jnp.concatenate(sides, axis=1)

    def bin_of(shape):
        r = lax.broadcasted_iota(jnp.int32, shape, 0)
        return blk * bins - HALO + r + jnp.where(r < seg_a, 0, chan * 2 * bins - seg_a)

    bin_p = bin_of((rows, 128))
    ok_p = (bin_p >= 0) & (bin_p < feature_len)
    in_p = (bin_p >= 0) & (bin_p < total)

    def keep(mask, value):
        return jnp.concatenate(
            [
                jnp.where(mask, value[:, at : at + 128], 0.0)
                for at in range(0, value.shape[1], 128)
            ],
            axis=1,
        )

    x = keep(ok_p, x)

    def layer(h, level):
        e = 2 ** (level + 1)
        taps = [
            pltpu.roll(h, e, 0).astype(jnp.bfloat16),
            h.astype(jnp.bfloat16),
            pltpu.roll(h, rows - e, 0).astype(jnp.bfloat16),
        ]
        parts = []
        for side in range(2):
            acc = jnp.dot(taps[0], wts[side, level, 0], preferred_element_type=jnp.float32)
            for t in (1, 2):
                acc += jnp.dot(taps[t], wts[side, level, t], preferred_element_type=jnp.float32)
            bias = cbias[side, level : level + 1].astype(jnp.float32)
            parts.append(jax.nn.relu(acc + bias))
        return (h + jnp.concatenate(parts, axis=1)).astype(jnp.bfloat16).astype(jnp.float32)

    h = layer(x, 0)
    h = keep(in_p, h)
    locals_[6].wait()
    wait_partner(5)
    h = layer(h, 1)
    proj = (
        (jnp.dot(h.astype(jnp.bfloat16), pw4[...], preferred_element_type=jnp.float32) + proj_b)
        .astype(jnp.bfloat16)
        .astype(jnp.float32)
    )
    pa_ref[...] = jnp.where(ok_p[:seg_a], proj[:seg_a, :128], NEG)
    pb = jnp.where(ok_p[seg_a:], proj[seg_a:, 128:], NEG)
    for v in range(3):
        pb_ref[v] = pb + gate_ref[v]

    cols = 2 * bins
    n_tile = cols // 64
    low_lane = lax.broadcasted_iota(jnp.int32, (16, 128), 1) < F2
    for v in range(3):
        for t in range(n_tile):
            for p in range(2):
                taps = [
                    pb_ref[v, pl.ds(HALO + 64 * t + p + (SLOT[k] - 1) * D2, 16, stride=4), :]
                    for k in range(4)
                ]
                for k in range(2):
                    both = jnp.where(low_lane, taps[2 * k], taps[2 * k + 1])
                    pb4_ref[v, t, 16 * p : 16 * p + 16, 128 * k : 128 * k + 128] = both.astype(
                        jnp.bfloat16
                    )

    def build(r, t):
        v = 0 if r < D2 else (2 if r >= bins + D2 else 1)
        at = r + HALO - D2
        row = jnp.broadcast_to(pa_ref[at : at + 1, :], (16, 128)).astype(jnp.bfloat16)
        row = jnp.concatenate([jnp.concatenate([row, row], axis=1)] * 2, axis=0)
        q_ref[r, t] = jnp.maximum(pb4_ref[v, t] + row, jnp.bfloat16(0))

    out_row = lax.broadcasted_iota(jnp.int32, (8, cols), 0)
    out_lane = lax.broadcasted_iota(jnp.int32, (8, cols), 1) + chan * cols
    live_row = live_cols(0, out_lane // bins)
    live_row = jnp.where(blk * bins + out_lane < feature_len, live_row, 0)

    pbn_ref[...] = pb_ref[1, HALO : HALO + cols, :].astype(jnp.bfloat16)
    low_row = lax.broadcasted_iota(jnp.int32, (1, 128), 1) < F2
    bases = (0, 1, 4, 5)

    def conv(first):
        windows = jnp.concatenate(
            [
                jnp.concatenate([q_ref[8 * g + a + 2 * j, t] for j in range(4)], axis=1)
                for g in range(first, first + TILE_STEP)
                for t in range(n_tile)
                for a in bases
            ],
            axis=0,
        )
        wide = jnp.dot(windows, mapw[...], preferred_element_type=jnp.float32)
        at = 0
        for g in range(first, first + TILE_STEP):
            for t in range(n_tile):
                for j in range(4):
                    for p in range(2):
                        for k in range(2):
                            wide_ref[4 * g + j, pl.ds(64 * t + p + 2 * k, 16, stride=4), :] = wide[
                                at : at + 16, 128 * k : 128 * k + 128
                            ]
                        at += 16

    def finish(first):
        for g in range(first, first + TILE_STEP):
            sides = []
            for j, a in enumerate(bases):
                acc = jax.nn.relu(wide_ref[4 * g + j] + bias_map).astype(jnp.bfloat16)
                at = 8 * g + a + HALO
                row = jnp.where(low_row, pa_ref[at : at + 1, :], pa_ref[at + D2 : at + D2 + 1, :])
                row = jnp.broadcast_to(row, (16, 128)).astype(jnp.bfloat16)
                row = jnp.concatenate([row] * (cols // 16), axis=0)
                sides.append(acc + jnp.maximum(pbn_ref[...] + row, jnp.bfloat16(0)))
            mixed = jnp.concatenate(sides, axis=1)
            result = lax.dot_general(head_mat, mixed, NT, preferred_element_type=jnp.float32)
            live = jnp.where(blk * bins + 8 * g + out_row < feature_len, live_row, 0)
            out_ref[8 * g : 8 * g + 8, :] = jnp.where(live > 0, result, 0.0)

    done = 0
    for first in range(0, bins // 8, TILE_STEP):
        upto = 8 * (first + TILE_STEP) + 2 * D2
        for r in range(done, upto):
            for t in range(n_tile):
                build(r, t)
        done = upto
        conv(first)
        if first > 0:
            finish(first - TILE_STEP)
    finish(bins // 8 - TILE_STEP)


def local(
    features,
    chrom_len,
    band_mask,
    conv_weight,
    conv_bias,
    proj_weight,
    proj_bias,
    map_weight,
    map_bias,
    head_weight,
):
    import functools

    bins, half = features.shape
    n_blk = lax.axis_size("blk")
    bf = jnp.bfloat16
    any_spec = pl.BlockSpec(memory_space=pltpu.HBM)
    smem = pl.BlockSpec(memory_space=pltpu.SMEM)
    ho = map_weight.shape[2]
    return pl.pallas_call(
        functools.partial(kernel, n_blk, bins),
        out_shape=pltpu.VMEM((bins, 2 * bins), jnp.float32),
        in_specs=[smem] + [any_spec] * 9,
        out_specs=pl.BlockSpec(memory_space=pltpu.VMEM),
        scratch_shapes=[
            pltpu.VMEM((2, 3, bins, half), bf),
            pltpu.VMEM((2, 16, half // 2), bf),
            pltpu.VMEM((2, 4, 16, half // 2), bf),
            pltpu.VMEM((2,) + conv_weight.shape, bf),
            pltpu.VMEM((2,) + conv_bias.shape, bf),
            pltpu.VMEM(proj_weight.shape, bf),
            pltpu.VMEM((1, 2 * F2), bf),
            pltpu.VMEM((2,) + map_weight.shape, bf),
            pltpu.VMEM((2, 1, ho), bf),
            pltpu.VMEM((2, 1, ho), bf),
            pltpu.VMEM((256, 1024), bf),
            pltpu.VMEM((1024, 256), bf),
            pltpu.VMEM((proj_weight.shape[0], 256), bf),
            pltpu.VMEM((bins + 2 * HALO, 128), jnp.float32),
            pltpu.VMEM((3, 2 * bins + 2 * HALO, 128), jnp.float32),
            pltpu.VMEM((3, 2, 32, 256), bf),
            pltpu.VMEM((bins + 2 * D2, 2, 32, 256), bf),
            pltpu.VMEM((3, 2 * bins + 2 * HALO, 128), jnp.float32),
            pltpu.SMEM((BAND + 1, n_blk), jnp.int32),
            pltpu.VMEM((bins // 2, 2 * bins, 128), jnp.float32),
            pltpu.VMEM((2 * bins, 128), bf),
            pltpu.SemaphoreType.DMA((9,)),
            pltpu.SemaphoreType.DMA((9, 2)),
            pltpu.SemaphoreType.DMA((7,)),
            pltpu.SemaphoreType.DMA((7,)),
            pltpu.SemaphoreType.DMA((10,)),
        ],
        compiler_params=pltpu.CompilerParams(
            collective_id=0, has_side_effects=True, vmem_limit_bytes=60 * 2**20
        ),
        name="contact",
    )(
        chrom_len,
        band_mask.T,
        features,
        conv_weight,
        conv_bias,
        proj_weight,
        proj_bias.reshape(1, -1),
        map_weight,
        map_bias.reshape(1, -1),
        head_weight.reshape(1, -1),
    )


def solution(mesh):
    return jax.shard_map(
        local,
        mesh=mesh,
        in_specs=(
            P(("dp", "blk"), "chan"),
            P("dp"),
            P("dp", None),
            P(None, None, None, "chan"),
            P(None, "chan"),
            P(),
            P(),
            P(None, None, "chan", None),
            P("chan"),
            P("chan"),
        ),
        out_specs=P(("dp", "blk"), "chan"),
        check_vma=False,
    )
```

```python
import jax
import jax.numpy as jnp
from jax import lax
from jax.experimental import pallas as pl
from jax.experimental.pallas import tpu as pltpu
from jax.sharding import PartitionSpec as P

F2 = 64
BAND = 3
D2 = 2
NEG = float("-inf")
HALO = 8
TILE_STEP = 4
SLOT = (1, 2, 0, 3)
NT = (((1,), (1,)), ((), ()))


PLAN = {
    -1: ((0, "last", 0), (1, "last", 0)),
    1: ((1, "both", 1), (0, "first", 1), (0, "full", 2)),
    2: ((1, "full", 1), (0, "first", 3)),
    3: ((1, "full", 2),),
    4: ((1, "first", 3),),
}
ORDER = (4,3,2,-1,1)
SIZE = {"first": 8, "last": 8, "both": 16, "full": 64}


def kernel(
    n_blk,
    bins,
    len_ref,
    mask_hbm,
    x_hbm,
    cw_hbm,
    cb_hbm,
    pw_hbm,
    pb_hbm,
    mw_hbm,
    mb_hbm,
    hw_hbm,
    out_ref,
    feat,
    rim_out,
    rim_in,
    wts,
    cbias,
    pwt,
    pbias,
    mwt,
    small,
    mapt,
    mapw,
    pw4,
    pa_ref,
    pb_ref,
    pb4_ref,
    q_ref,
    gate_ref,
    mask_ref,
    wide_ref,
    pbn_ref,
    send_sem,
    recv_sem,
    give_sem,
    pair_sem,
    loc_sem,
):
    dp = lax.axis_index("dp")
    blk = lax.axis_index("blk")
    chan = lax.axis_index("chan")
    other = 1 - chan
    half = x_hbm.shape[1]

    def dev(b, c):
        return (dp, b, c)

    barrier = pltpu.get_barrier_semaphore()

    def signal(b, c):
        pl.semaphore_signal(
            barrier, inc=1, device_id=dev(b, c), device_id_type=pl.DeviceIdType.MESH
        )

    signal(blk, other)
    for d in (-1, 1, 2, 3, 4):
        inside = (blk + d >= 0) & (blk + d < n_blk)
        if d >= 3:
            inside = inside & (chan == 1)

        @pl.when(inside)
        def _(d=d):
            signal(blk + d, 0)
            signal(blk + d, 1)

    def joined(ref, sem):
        pltpu.make_async_copy(ref, ref, sem).wait()

    x_local = pltpu.make_async_copy(x_hbm, feat.at[chan, 0], loc_sem.at[0])
    mask_local = pltpu.make_async_copy(mask_hbm, mask_ref, loc_sem.at[1])
    pw_local = pltpu.make_async_copy(pw_hbm, pwt, loc_sem.at[2])
    pb_local = pltpu.make_async_copy(pb_hbm, pbias, loc_sem.at[3])
    for copy in (x_local, mask_local, pw_local, pb_local):
        copy.start()
    for src, dst, slot in (
        (mw_hbm, mwt.at[chan], 0),
        (mb_hbm, small.at[0, chan], 1),
        (hw_hbm, small.at[1, chan], 1),
        (cb_hbm, cbias.at[chan], 2),
        (cw_hbm.at[0], wts.at[chan, 0], 3),
        (cw_hbm.at[1], wts.at[chan, 1], 4),
    ):
        pltpu.make_async_copy(src, dst, pair_sem.at[slot]).start()

    x_local.wait()
    for side in range(2):
        edge = feat[chan, 0, 0:16] if side == 0 else feat[chan, 0, bins - 16 : bins]
        edge = edge.astype(jnp.float32)[8 * side : 8 * side + 8]
        rim_out[side] = jnp.concatenate([edge[:, :128], edge[:, 128:]], axis=0).astype(
            jnp.bfloat16
        )

    def has(d):
        return jnp.where((blk - d >= 0) & (blk - d < n_blk), 1, 0)

    pl.semaphore_wait(barrier, 1 + 2 * has(-1) + 2 * has(1) + 2 * has(2) + has(3) + has(4))

    def feature_copy(d, n, sender):
        rc, kind, slot = PLAN[d][n]
        if kind == "full":
            src, dst = feat.at[sender, 0], feat.at[sender, slot]
        elif kind == "both":
            src, dst = rim_out, rim_in.at[sender, pl.ds(slot, 2)]
        else:
            src, dst = rim_out.at[0 if kind == "first" else 1], rim_in.at[sender, slot]
        return pltpu.make_async_remote_copy(
            src_ref=src,
            dst_ref=dst,
            send_sem=send_sem.at[max(d, 0)],
            recv_sem=recv_sem.at[max(d, 0)],
            device_id=dev(blk - d, rc),
            device_id_type=pl.DeviceIdType.MESH,
        )

    for d in ORDER:

        @pl.when((blk - d >= 0) & (blk - d < n_blk))
        def _(d=d):
            for n in range(len(PLAN[d])):
                feature_copy(d, n, chan).start()

    for src, dst, send, recv in (
        (mw_hbm, mwt.at[chan], give_sem.at[0], pair_sem.at[0]),
        (mb_hbm, small.at[0, chan], give_sem.at[1], pair_sem.at[1]),
        (hw_hbm, small.at[1, chan], give_sem.at[1], pair_sem.at[1]),
        (cb_hbm, cbias.at[chan], give_sem.at[2], pair_sem.at[2]),
        (x_hbm, feat.at[chan, 0], give_sem.at[3], loc_sem.at[4]),
        (cw_hbm.at[0], wts.at[chan, 0], give_sem.at[4], pair_sem.at[3]),
        (cw_hbm.at[1], wts.at[chan, 1], give_sem.at[4], pair_sem.at[4]),
    ):
        pltpu.make_async_remote_copy(
            src_ref=src,
            dst_ref=dst,
            send_sem=send,
            recv_sem=recv,
            device_id=dev(blk, other),
            device_id_type=pl.DeviceIdType.MESH,
        ).start()

    mapt[...] = jnp.zeros_like(mapt)
    joined(mwt, pair_sem.at[0])
    joined(small, pair_sem.at[1])
    joined(cbias, pair_sem.at[2])
    ho = mw_hbm.shape[2]
    for side in range(2):
        for s in range(3):
            for t in range(3):
                block = mwt[side, s, t]
                for k1 in range(2):
                    for k2 in range(2):
                        r0 = (2 * k2 + k1) * F2 + side * ho
                        c0 = (s + k1) * 256 + SLOT.index(t + k2) * F2
                        mapt[r0 : r0 + ho, c0 : c0 + F2] = block
    mapw[...] = jnp.transpose(mapt[...])
    pw_local.wait()
    pb_local.wait()
    for part in range(2):
        block = pwt[:, part * F2 : (part + 1) * F2]
        for twice in range(2):
            at = (2 * part + twice) * F2
            pw4[:, at : at + F2] = block
    proj_b = pbias[...].astype(jnp.float32)
    proj_b = jnp.concatenate(
        [proj_b[:, :F2], proj_b[:, :F2], proj_b[:, F2:], proj_b[:, F2:]], axis=1
    )
    sel_row = lax.broadcasted_iota(jnp.int32, (ho, 512), 0)
    sel_lane = lax.broadcasted_iota(jnp.int32, (ho, 512), 1) % F2
    bias_row = jnp.zeros((1, 512), jnp.float32)
    head_row = jnp.zeros((1, 512), jnp.float32)
    for side in range(2):
        spread = jnp.where(sel_lane == sel_row + side * ho, 1.0, 0.0).astype(jnp.bfloat16)
        bias_row += jnp.dot(small[0, side], spread, preferred_element_type=jnp.float32)
        head_row += jnp.dot(small[1, side], spread, preferred_element_type=jnp.float32)
    bias_map = bias_row[:, :128]
    h_row = lax.broadcasted_iota(jnp.int32, (8, 512), 0)
    h_lane = lax.broadcasted_iota(jnp.int32, (8, 512), 1) // F2
    h_want = (h_lane // 4) * 4 + (h_lane // 2) % 2 + 2 * (h_lane % 2)
    head_mat = jnp.where(
        h_row == h_want, jnp.broadcast_to(head_row, (8, 512)), 0.0
    ).astype(jnp.bfloat16)
    mask_local.wait()

    seg_a = bins + 2 * HALO
    seg_b = 2 * bins + 2 * HALO
    rows = seg_a + seg_b
    sub_b = lax.broadcasted_iota(jnp.int32, (seg_b, 128), 0)
    col_block = (chan * 2 * bins - HALO + bins + sub_b) // bins - 1

    def live_cols(block_shift, col_blk):
        at = blk + block_shift
        inside = (at >= 0) & (at < n_blk)
        at = lax.rem(at + n_blk, n_blk)
        live = jnp.zeros(col_blk.shape, jnp.int32)
        for o in range(BAND + 1):
            flag = jnp.where(inside, mask_ref[o, at], 0)
            live = jnp.where(col_blk - block_shift == o, flag, live)
        return live

    for v in range(3):
        gate_ref[v] = jnp.where(live_cols(v - 1, col_block) > 0, 0.0, NEG)

    feature_len = len_ref[0]
    total = n_blk * bins
    def received(entries, copies, sem):
        total = copies * sum(SIZE[kind] for _, kind, _ in entries)
        split = 1 if total <= 128 else 2
        joined(wide_ref.at[0:split, 0 : total // split], sem)

    joined(mwt.at[0], give_sem.at[0])
    joined(small.at[:, 0], give_sem.at[1])
    joined(cbias.at[0], give_sem.at[2])
    joined(feat.at[0, 0], give_sem.at[3])
    joined(wts.at[0], give_sem.at[4])
    for d in PLAN:

        @pl.when((blk - d >= 0) & (blk - d < n_blk))
        def _(d=d):
            received(PLAN[d], 1, send_sem.at[max(d, 0)])

    joined(feat.at[0, 0], loc_sem.at[4])
    for d in PLAN:
        for rc in range(2):
            mine = [entry for entry in PLAN[d] if entry[0] == rc]
            if not mine:
                continue

            @pl.when((blk + d >= 0) & (blk + d < n_blk) & (chan == rc))
            def _(d=d, mine=mine):
                received(mine, 2, recv_sem.at[max(d, 0)])

    joined(wts.at[:, 0], pair_sem.at[3])

    left = jnp.where(chan == 0, 0, 2)
    near = jnp.where(chan == 0, 0, 1)
    sides = []
    for side in range(2):
        edges = [rim_in[side, k].astype(jnp.float32) for k in (0, 1, left, 3)]
        edges = [jnp.concatenate([edge[:8], edge[8:]], axis=1) for edge in edges]
        block = [feat[side, k].astype(jnp.float32) for k in (0, near, 2)]
        sides.append(
            jnp.concatenate(
                [edges[0], block[0], edges[1], edges[2], block[1], block[2], edges[3]], axis=0
            )
        )
    x = jnp.concatenate(sides, axis=1)

    def bin_of(shape):
        r = lax.broadcasted_iota(jnp.int32, shape, 0)
        return blk * bins - HALO + r + jnp.where(r < seg_a, 0, chan * 2 * bins - seg_a)

    bin_p = bin_of((rows, 128))
    ok_p = (bin_p >= 0) & (bin_p < feature_len)
    in_p = (bin_p >= 0) & (bin_p < total)

    def keep(mask, value):
        return jnp.concatenate(
            [
                jnp.where(mask, value[:, at : at + 128], 0.0)
                for at in range(0, value.shape[1], 128)
            ],
            axis=1,
        )

    x = keep(ok_p, x)

    def layer(h, level):
        e = 2 ** (level + 1)
        taps = [
            pltpu.roll(h, e, 0).astype(jnp.bfloat16),
            h.astype(jnp.bfloat16),
            pltpu.roll(h, rows - e, 0).astype(jnp.bfloat16),
        ]
        parts = []
        for side in range(2):
            acc = jnp.dot(taps[0], wts[side, level, 0], preferred_element_type=jnp.float32)
            for t in (1, 2):
                acc += jnp.dot(taps[t], wts[side, level, t], preferred_element_type=jnp.float32)
            bias = cbias[side, level : level + 1].astype(jnp.float32)
            parts.append(jax.nn.relu(acc + bias))
        return (h + jnp.concatenate(parts, axis=1)).astype(jnp.bfloat16).astype(jnp.float32)

    h = layer(x, 0)
    h = keep(in_p, h)
    joined(wts.at[:, 1], pair_sem.at[4])
    h = layer(h, 1)
    proj = (
        (jnp.dot(h.astype(jnp.bfloat16), pw4[...], preferred_element_type=jnp.float32) + proj_b)
        .astype(jnp.bfloat16)
        .astype(jnp.float32)
    )
    pa_ref[...] = jnp.where(ok_p[:seg_a], proj[:seg_a, :128], NEG)
    pb = jnp.where(ok_p[seg_a:], proj[seg_a:, 128:], NEG)
    for v in range(3):
        pb_ref[v] = pb + gate_ref[v]

    cols = 2 * bins
    n_tile = cols // 64
    low_lane = lax.broadcasted_iota(jnp.int32, (16, 128), 1) < F2
    for v in range(3):
        for t in range(n_tile):
            for p in range(2):
                taps = [
                    pb_ref[v, pl.ds(HALO + 64 * t + p + (SLOT[k] - 1) * D2, 16, stride=4), :]
                    for k in range(4)
                ]
                for k in range(2):
                    both = jnp.where(low_lane, taps[2 * k], taps[2 * k + 1])
                    pb4_ref[v, t, 16 * p : 16 * p + 16, 128 * k : 128 * k + 128] = both.astype(
                        jnp.bfloat16
                    )

    def build(r, t):
        v = 0 if r < D2 else (2 if r >= bins + D2 else 1)
        at = r + HALO - D2
        row = jnp.broadcast_to(pa_ref[at : at + 1, :], (16, 128)).astype(jnp.bfloat16)
        row = jnp.concatenate([jnp.concatenate([row, row], axis=1)] * 2, axis=0)
        q_ref[r, t] = jnp.maximum(pb4_ref[v, t] + row, jnp.bfloat16(0))

    out_row = lax.broadcasted_iota(jnp.int32, (8, cols), 0)
    out_lane = lax.broadcasted_iota(jnp.int32, (8, cols), 1) + chan * cols
    live_row = live_cols(0, out_lane // bins)
    live_row = jnp.where(blk * bins + out_lane < feature_len, live_row, 0)

    pbn_ref[...] = pb_ref[1, HALO : HALO + cols, :].astype(jnp.bfloat16)
    low_row = lax.broadcasted_iota(jnp.int32, (1, 128), 1) < F2
    bases = (0, 1, 4, 5)

    def conv(first):
        windows = jnp.concatenate(
            [
                jnp.concatenate([q_ref[8 * g + a + 2 * j, t] for j in range(4)], axis=1)
                for g in range(first, first + TILE_STEP)
                for t in range(n_tile)
                for a in bases
            ],
            axis=0,
        )
        wide = jnp.dot(windows, mapw[...], preferred_element_type=jnp.float32)
        at = 0
        for g in range(first, first + TILE_STEP):
            for t in range(n_tile):
                for j in range(4):
                    for p in range(2):
                        for k in range(2):
                            wide_ref[4 * g + j, pl.ds(64 * t + p + 2 * k, 16, stride=4), :] = wide[
                                at : at + 16, 128 * k : 128 * k + 128
                            ]
                        at += 16

    def finish(first):
        for g in range(first, first + TILE_STEP):
            sides = []
            for j, a in enumerate(bases):
                acc = jax.nn.relu(wide_ref[4 * g + j] + bias_map).astype(jnp.bfloat16)
                at = 8 * g + a + HALO
                row = jnp.where(low_row, pa_ref[at : at + 1, :], pa_ref[at + D2 : at + D2 + 1, :])
                row = jnp.broadcast_to(row, (16, 128)).astype(jnp.bfloat16)
                row = jnp.concatenate([row] * (cols // 16), axis=0)
                sides.append(acc + jnp.maximum(pbn_ref[...] + row, jnp.bfloat16(0)))
            mixed = jnp.concatenate(sides, axis=1)
            result = lax.dot_general(head_mat, mixed, NT, preferred_element_type=jnp.float32)
            live = jnp.where(blk * bins + 8 * g + out_row < feature_len, live_row, 0)
            out_ref[8 * g : 8 * g + 8, :] = jnp.where(live > 0, result, 0.0)

    done = 0
    for first in range(0, bins // 8, TILE_STEP):
        upto = 8 * (first + TILE_STEP) + 2 * D2
        for r in range(done, upto):
            for t in range(n_tile):
                build(r, t)
        done = upto
        conv(first)
        if first > 0:
            finish(first - TILE_STEP)
    finish(bins // 8 - TILE_STEP)


def local(
    features,
    chrom_len,
    band_mask,
    conv_weight,
    conv_bias,
    proj_weight,
    proj_bias,
    map_weight,
    map_bias,
    head_weight,
):
    import functools

    bins, half = features.shape
    n_blk = lax.axis_size("blk")
    bf = jnp.bfloat16
    any_spec = pl.BlockSpec(memory_space=pltpu.HBM)
    smem = pl.BlockSpec(memory_space=pltpu.SMEM)
    ho = map_weight.shape[2]
    return pl.pallas_call(
        functools.partial(kernel, n_blk, bins),
        out_shape=pltpu.VMEM((bins, 2 * bins), jnp.float32),
        in_specs=[smem] + [any_spec] * 9,
        out_specs=pl.BlockSpec(memory_space=pltpu.VMEM),
        scratch_shapes=[
            pltpu.VMEM((2, 3, bins, half), bf),
            pltpu.VMEM((2, 16, half // 2), bf),
            pltpu.VMEM((2, 4, 16, half // 2), bf),
            pltpu.VMEM((2,) + conv_weight.shape, bf),
            pltpu.VMEM((2,) + conv_bias.shape, bf),
            pltpu.VMEM(proj_weight.shape, bf),
            pltpu.VMEM((1, 2 * F2), bf),
            pltpu.VMEM((2,) + map_weight.shape, bf),
            pltpu.VMEM((2, 2, 1, ho), bf),
            pltpu.VMEM((256, 1024), bf),
            pltpu.VMEM((1024, 256), bf),
            pltpu.VMEM((proj_weight.shape[0], 256), bf),
            pltpu.VMEM((bins + 2 * HALO, 128), jnp.float32),
            pltpu.VMEM((3, 2 * bins + 2 * HALO, 128), jnp.float32),
            pltpu.VMEM((3, 2, 32, 256), bf),
            pltpu.VMEM((bins + 2 * D2, 2, 32, 256), bf),
            pltpu.VMEM((3, 2 * bins + 2 * HALO, 128), jnp.float32),
            pltpu.SMEM((BAND + 1, n_blk), jnp.int32),
            pltpu.VMEM((bins // 2, 2 * bins, 128), jnp.float32),
            pltpu.VMEM((2 * bins, 128), bf),
            pltpu.SemaphoreType.DMA((5,)),
            pltpu.SemaphoreType.DMA((5,)),
            pltpu.SemaphoreType.DMA((5,)),
            pltpu.SemaphoreType.DMA((5,)),
            pltpu.SemaphoreType.DMA((5,)),
        ],
        compiler_params=pltpu.CompilerParams(
            collective_id=0, has_side_effects=True, vmem_limit_bytes=60 * 2**20
        ),
        name="contact",
    )(
        chrom_len,
        band_mask.T,
        features,
        conv_weight,
        conv_bias,
        proj_weight,
        proj_bias.reshape(1, -1),
        map_weight,
        map_bias.reshape(1, -1),
        head_weight.reshape(1, -1),
    )


def solution(mesh):
    return jax.shard_map(
        local,
        mesh=mesh,
        in_specs=(
            P(("dp", "blk"), "chan"),
            P("dp"),
            P("dp", None),
            P(None, None, None, "chan"),
            P(None, "chan"),
            P(),
            P(),
            P(None, None, "chan", None),
            P("chan"),
            P("chan"),
        ),
        out_specs=P(("dp", "blk"), "chan"),
        check_vma=False,
    )
```

```python
import jax
import jax.numpy as jnp
from jax import lax
from jax.experimental import pallas as pl
from jax.experimental.pallas import tpu as pltpu
from jax.sharding import PartitionSpec as P

F2 = 64
BAND = 3
D2 = 2
NEG = float("-inf")
HALO = 8
TILE_STEP = 4
SLOT = (1, 2, 0, 3)
NT = (((1,), (1,)), ((), ()))


PLAN = {
    -1: ((0, "last", 0), (1, "last", 0)),
    1: ((1, "both", 1), (0, "first", 1), (0, "full", 2)),
    2: ((1, "full", 1), (0, "first", 3)),
    3: ((1, "full", 2),),
    4: ((1, "first", 3),),
}
ORDER = (4,3,2,-1,1)
SIZE = {"first": 8, "last": 8, "both": 16, "full": 64}


def kernel(
    n_blk,
    bins,
    len_ref,
    mask_hbm,
    x_hbm,
    cw_hbm,
    cb_hbm,
    pw_hbm,
    pb_hbm,
    mw_hbm,
    mb_hbm,
    hw_hbm,
    out_ref,
    feat,
    rim_out,
    rim_in,
    wts,
    cbias,
    pwt,
    pbias,
    mwt,
    small,
    mapt,
    mapw,
    pw4,
    pa_ref,
    pb_ref,
    pb4_ref,
    q_ref,
    gate_ref,
    mask_ref,
    wide_ref,
    pbn_ref,
    send_sem,
    recv_sem,
    give_sem,
    pair_sem,
    loc_sem,
):
    dp = lax.axis_index("dp")
    blk = lax.axis_index("blk")
    chan = lax.axis_index("chan")
    other = 1 - chan
    half = x_hbm.shape[1]

    def dev(b, c):
        return (dp, b, c)

    barrier = pltpu.get_barrier_semaphore()

    def signal(b, c):
        pl.semaphore_signal(
            barrier, inc=1, device_id=dev(b, c), device_id_type=pl.DeviceIdType.MESH
        )

    signal(blk, other)
    for d in (-1, 1, 2, 3, 4):
        inside = (blk + d >= 0) & (blk + d < n_blk)
        if d >= 3:
            inside = inside & (chan == 1)

        @pl.when(inside)
        def _(d=d):
            signal(blk + d, 0)
            signal(blk + d, 1)

    def joined(ref, sem):
        pltpu.make_async_copy(ref, ref, sem).wait()

    x_local = pltpu.make_async_copy(x_hbm, feat.at[chan, 0], loc_sem.at[0])
    mask_local = pltpu.make_async_copy(mask_hbm, mask_ref, loc_sem.at[1])
    pw_local = pltpu.make_async_copy(pw_hbm, pwt, loc_sem.at[2])
    pb_local = pltpu.make_async_copy(pb_hbm, pbias, loc_sem.at[3])
    for copy in (x_local, mask_local, pw_local, pb_local):
        copy.start()
    for src, dst, slot in (
        (mw_hbm, mwt.at[chan], 0),
        (mb_hbm, small.at[0, chan], 1),
        (hw_hbm, small.at[1, chan], 1),
        (cb_hbm, cbias.at[chan], 2),
        (cw_hbm.at[0], wts.at[chan, 0], 3),
        (cw_hbm.at[1], wts.at[chan, 1], 4),
    ):
        pltpu.make_async_copy(src, dst, pair_sem.at[slot]).start()

    x_local.wait()
    for side in range(2):
        edge = feat[chan, 0, 0:16] if side == 0 else feat[chan, 0, bins - 16 : bins]
        edge = edge.astype(jnp.float32)[8 * side : 8 * side + 8]
        rim_out[side] = jnp.concatenate([edge[:, :128], edge[:, 128:]], axis=0).astype(
            jnp.bfloat16
        )

    def has(d):
        return jnp.where((blk - d >= 0) & (blk - d < n_blk), 1, 0)

    pl.semaphore_wait(barrier, 1 + 2 * has(-1) + 2 * has(1) + 2 * has(2) + has(3) + has(4))

    def feature_copy(d, n, sender):
        rc, kind, slot = PLAN[d][n]
        if kind == "full":
            src, dst = feat.at[sender, 0], feat.at[sender, slot]
        elif kind == "both":
            src, dst = rim_out, rim_in.at[sender, pl.ds(slot, 2)]
        else:
            src, dst = rim_out.at[0 if kind == "first" else 1], rim_in.at[sender, slot]
        return pltpu.make_async_remote_copy(
            src_ref=src,
            dst_ref=dst,
            send_sem=send_sem.at[max(d, 0)],
            recv_sem=recv_sem.at[max(d, 0)],
            device_id=dev(blk - d, rc),
            device_id_type=pl.DeviceIdType.MESH,
        )

    for d in ORDER:

        @pl.when((blk - d >= 0) & (blk - d < n_blk))
        def _(d=d):
            for n in range(len(PLAN[d])):
                feature_copy(d, n, chan).start()

    for src, dst, send, recv in (
        (mw_hbm, mwt.at[chan], give_sem.at[0], pair_sem.at[0]),
        (mb_hbm, small.at[0, chan], give_sem.at[1], pair_sem.at[1]),
        (hw_hbm, small.at[1, chan], give_sem.at[1], pair_sem.at[1]),
        (cb_hbm, cbias.at[chan], give_sem.at[2], pair_sem.at[2]),
        (x_hbm, feat.at[chan, 0], give_sem.at[3], loc_sem.at[4]),
        (cw_hbm.at[0], wts.at[chan, 0], give_sem.at[4], pair_sem.at[3]),
        (cw_hbm.at[1], wts.at[chan, 1], give_sem.at[4], pair_sem.at[4]),
    ):
        pltpu.make_async_remote_copy(
            src_ref=src,
            dst_ref=dst,
            send_sem=send,
            recv_sem=recv,
            device_id=dev(blk, other),
            device_id_type=pl.DeviceIdType.MESH,
        ).start()

    mapt[...] = jnp.zeros_like(mapt)
    joined(mwt, pair_sem.at[0])
    joined(small, pair_sem.at[1])
    joined(cbias, pair_sem.at[2])
    ho = mw_hbm.shape[2]
    for side in range(2):
        for s in range(3):
            for t in range(3):
                block = mwt[side, s, t]
                for k1 in range(2):
                    for k2 in range(2):
                        r0 = (2 * k2 + k1) * F2 + side * ho
                        c0 = (s + k1) * 256 + SLOT.index(t + k2) * F2
                        mapt[r0 : r0 + ho, c0 : c0 + F2] = block
    mapw[...] = jnp.transpose(mapt[...])
    pw_local.wait()
    pb_local.wait()
    for part in range(2):
        block = pwt[:, part * F2 : (part + 1) * F2]
        for twice in range(2):
            at = (2 * part + twice) * F2
            pw4[:, at : at + F2] = block
    proj_b = pbias[...].astype(jnp.float32)
    proj_b = jnp.concatenate(
        [proj_b[:, :F2], proj_b[:, :F2], proj_b[:, F2:], proj_b[:, F2:]], axis=1
    )
    sel_row = lax.broadcasted_iota(jnp.int32, (ho, 512), 0)
    sel_lane = lax.broadcasted_iota(jnp.int32, (ho, 512), 1) % F2
    bias_row = jnp.zeros((1, 512), jnp.float32)
    head_row = jnp.zeros((1, 512), jnp.float32)
    for side in range(2):
        spread = jnp.where(sel_lane == sel_row + side * ho, 1.0, 0.0).astype(jnp.bfloat16)
        bias_row += jnp.dot(small[0, side], spread, preferred_element_type=jnp.float32)
        head_row += jnp.dot(small[1, side], spread, preferred_element_type=jnp.float32)
    bias_map = bias_row[:, :128]
    h_row = lax.broadcasted_iota(jnp.int32, (8, 512), 0)
    h_lane = lax.broadcasted_iota(jnp.int32, (8, 512), 1) // F2
    h_want = (h_lane // 4) * 4 + (h_lane // 2) % 2 + 2 * (h_lane % 2)
    head_mat = jnp.where(
        h_row == h_want, jnp.broadcast_to(head_row, (8, 512)), 0.0
    ).astype(jnp.bfloat16)
    mask_local.wait()

    seg_a = bins + 2 * HALO
    seg_b = 2 * bins + 2 * HALO
    rows = seg_a + seg_b
    sub_b = lax.broadcasted_iota(jnp.int32, (seg_b, 128), 0)
    col_block = (chan * 2 * bins - HALO + bins + sub_b) // bins - 1

    def live_cols(block_shift, col_blk):
        at = blk + block_shift
        inside = (at >= 0) & (at < n_blk)
        at = lax.rem(at + n_blk, n_blk)
        live = jnp.zeros(col_blk.shape, jnp.int32)
        for o in range(BAND + 1):
            flag = jnp.where(inside, mask_ref[o, at], 0)
            live = jnp.where(col_blk - block_shift == o, flag, live)
        return live

    for v in range(3):
        gate_ref[v] = jnp.where(live_cols(v - 1, col_block) > 0, 0.0, NEG)

    feature_len = len_ref[0]
    total = n_blk * bins
    def received(entries, copies, sem):
        total = copies * sum(SIZE[kind] for _, kind, _ in entries)
        split = 1 if total <= 128 else 2
        joined(wide_ref.at[0:split, 0 : total // split], sem)

    joined(mwt.at[0], give_sem.at[0])
    joined(small.at[:, 0], give_sem.at[1])
    joined(cbias.at[0], give_sem.at[2])
    joined(feat.at[0, 0], give_sem.at[3])
    joined(wts.at[0], give_sem.at[4])
    for d in PLAN:

        @pl.when((blk - d >= 0) & (blk - d < n_blk))
        def _(d=d):
            received(PLAN[d], 1, send_sem.at[max(d, 0)])

    joined(feat.at[0, 0], loc_sem.at[4])
    for d in PLAN:
        for rc in range(2):
            mine = [entry for entry in PLAN[d] if entry[0] == rc]
            if not mine:
                continue

            @pl.when((blk + d >= 0) & (blk + d < n_blk) & (chan == rc))
            def _(d=d, mine=mine):
                received(mine, 2, recv_sem.at[max(d, 0)])

    joined(wts.at[:, 0], pair_sem.at[3])

    joined(wts.at[:, 1], pair_sem.at[4])

    def keep(mask, value):
        return jnp.concatenate(
            [
                jnp.where(mask, value[:, at : at + 128], 0.0)
                for at in range(0, value.shape[1], 128)
            ],
            axis=1,
        )

    def trunk(parts, first_rows):
        x = jnp.concatenate(
            [
                jnp.concatenate(
                    [
                        (
                            feat[side, k].astype(jnp.float32)
                            if kind == "block"
                            else jnp.concatenate(
                                [
                                    rim_in[side, k, 0:16].astype(jnp.float32)[:8],
                                    rim_in[side, k, 0:16].astype(jnp.float32)[8:],
                                ],
                                axis=1,
                            )
                        )
                        for kind, k in parts
                    ],
                    axis=0,
                )
                for side in range(2)
            ],
            axis=1,
        )
        rows = x.shape[0]
        r = lax.broadcasted_iota(jnp.int32, (rows, 128), 0)
        shift = jnp.where(r < first_rows, 0, chan * 2 * bins - first_rows)
        bin_p = blk * bins - HALO + r + shift
        ok_p = (bin_p >= 0) & (bin_p < feature_len)
        in_p = (bin_p >= 0) & (bin_p < total)

        def layer(h, level):
            e = 2 ** (level + 1)
            taps = [
                pltpu.roll(h, e, 0).astype(jnp.bfloat16),
                h.astype(jnp.bfloat16),
                pltpu.roll(h, rows - e, 0).astype(jnp.bfloat16),
            ]
            parts = []
            for side in range(2):
                acc = jnp.dot(taps[0], wts[side, level, 0], preferred_element_type=jnp.float32)
                for t in (1, 2):
                    acc += jnp.dot(taps[t], wts[side, level, t], preferred_element_type=jnp.float32)
                bias = cbias[side, level : level + 1].astype(jnp.float32)
                parts.append(jax.nn.relu(acc + bias))
            return (h + jnp.concatenate(parts, axis=1)).astype(jnp.bfloat16).astype(jnp.float32)

        h = layer(keep(ok_p, x), 0)
        h = layer(keep(in_p, h), 1)
        proj = (
            (jnp.dot(h.astype(jnp.bfloat16), pw4[...], preferred_element_type=jnp.float32) + proj_b)
            .astype(jnp.bfloat16)
            .astype(jnp.float32)
        )
        pa_ref[...] = jnp.where(ok_p[:seg_a], proj[:seg_a, :128], NEG)
        pb = jnp.where(ok_p[first_rows:], proj[first_rows:, 128:], NEG)
        for v in range(3):
            pb_ref[v] = pb + gate_ref[v]

    @pl.when(chan == 0)
    def _():
        trunk([("rim", 0), ("block", 0), ("block", 2), ("rim", 3)], 0)

    @pl.when(chan == 1)
    def _():
        own = [("rim", 0), ("block", 0), ("rim", 1)]
        trunk(own + [("rim", 2), ("block", 1), ("block", 2), ("rim", 3)], seg_a)

    cols = 2 * bins
    n_tile = cols // 64
    low_lane = lax.broadcasted_iota(jnp.int32, (16, 128), 1) < F2
    for v in range(3):
        for t in range(n_tile):
            for p in range(2):
                taps = [
                    pb_ref[v, pl.ds(HALO + 64 * t + p + (SLOT[k] - 1) * D2, 16, stride=4), :]
                    for k in range(4)
                ]
                for k in range(2):
                    both = jnp.where(low_lane, taps[2 * k], taps[2 * k + 1])
                    pb4_ref[v, t, 16 * p : 16 * p + 16, 128 * k : 128 * k + 128] = both.astype(
                        jnp.bfloat16
                    )

    def build(r, t):
        v = 0 if r < D2 else (2 if r >= bins + D2 else 1)
        at = r + HALO - D2
        row = jnp.broadcast_to(pa_ref[at : at + 1, :], (16, 128)).astype(jnp.bfloat16)
        row = jnp.concatenate([jnp.concatenate([row, row], axis=1)] * 2, axis=0)
        q_ref[r, t] = jnp.maximum(pb4_ref[v, t] + row, jnp.bfloat16(0))

    out_row = lax.broadcasted_iota(jnp.int32, (8, cols), 0)
    out_lane = lax.broadcasted_iota(jnp.int32, (8, cols), 1) + chan * cols
    live_row = live_cols(0, out_lane // bins)
    live_row = jnp.where(blk * bins + out_lane < feature_len, live_row, 0)

    pbn_ref[...] = pb_ref[1, HALO : HALO + cols, :].astype(jnp.bfloat16)
    low_row = lax.broadcasted_iota(jnp.int32, (1, 128), 1) < F2
    bases = (0, 1, 4, 5)

    def conv(first):
        windows = jnp.concatenate(
            [
                jnp.concatenate([q_ref[8 * g + a + 2 * j, t] for j in range(4)], axis=1)
                for g in range(first, first + TILE_STEP)
                for t in range(n_tile)
                for a in bases
            ],
            axis=0,
        )
        wide = jnp.dot(windows, mapw[...], preferred_element_type=jnp.float32)
        at = 0
        for g in range(first, first + TILE_STEP):
            for t in range(n_tile):
                for j in range(4):
                    for p in range(2):
                        for k in range(2):
                            wide_ref[4 * g + j, pl.ds(64 * t + p + 2 * k, 16, stride=4), :] = wide[
                                at : at + 16, 128 * k : 128 * k + 128
                            ]
                        at += 16

    def finish(first):
        for g in range(first, first + TILE_STEP):
            sides = []
            for j, a in enumerate(bases):
                acc = jax.nn.relu(wide_ref[4 * g + j] + bias_map).astype(jnp.bfloat16)
                at = 8 * g + a + HALO
                row = jnp.where(low_row, pa_ref[at : at + 1, :], pa_ref[at + D2 : at + D2 + 1, :])
                row = jnp.broadcast_to(row, (16, 128)).astype(jnp.bfloat16)
                row = jnp.concatenate([row] * (cols // 16), axis=0)
                sides.append(acc + jnp.maximum(pbn_ref[...] + row, jnp.bfloat16(0)))
            mixed = jnp.concatenate(sides, axis=1)
            result = lax.dot_general(head_mat, mixed, NT, preferred_element_type=jnp.float32)
            live = jnp.where(blk * bins + 8 * g + out_row < feature_len, live_row, 0)
            out_ref[8 * g : 8 * g + 8, :] = jnp.where(live > 0, result, 0.0)

    done = 0
    for first in range(0, bins // 8, TILE_STEP):
        upto = 8 * (first + TILE_STEP) + 2 * D2
        for r in range(done, upto):
            for t in range(n_tile):
                build(r, t)
        done = upto
        conv(first)
        if first > 0:
            finish(first - TILE_STEP)
    finish(bins // 8 - TILE_STEP)


def local(
    features,
    chrom_len,
    band_mask,
    conv_weight,
    conv_bias,
    proj_weight,
    proj_bias,
    map_weight,
    map_bias,
    head_weight,
):
    import functools

    bins, half = features.shape
    n_blk = lax.axis_size("blk")
    bf = jnp.bfloat16
    any_spec = pl.BlockSpec(memory_space=pltpu.HBM)
    smem = pl.BlockSpec(memory_space=pltpu.SMEM)
    ho = map_weight.shape[2]
    return pl.pallas_call(
        functools.partial(kernel, n_blk, bins),
        out_shape=pltpu.VMEM((bins, 2 * bins), jnp.float32),
        in_specs=[smem] + [any_spec] * 9,
        out_specs=pl.BlockSpec(memory_space=pltpu.VMEM),
        scratch_shapes=[
            pltpu.VMEM((2, 3, bins, half), bf),
            pltpu.VMEM((2, 16, half // 2), bf),
            pltpu.VMEM((2, 4, 16, half // 2), bf),
            pltpu.VMEM((2,) + conv_weight.shape, bf),
            pltpu.VMEM((2,) + conv_bias.shape, bf),
            pltpu.VMEM(proj_weight.shape, bf),
            pltpu.VMEM((1, 2 * F2), bf),
            pltpu.VMEM((2,) + map_weight.shape, bf),
            pltpu.VMEM((2, 2, 1, ho), bf),
            pltpu.VMEM((256, 1024), bf),
            pltpu.VMEM((1024, 256), bf),
            pltpu.VMEM((proj_weight.shape[0], 256), bf),
            pltpu.VMEM((bins + 2 * HALO, 128), jnp.float32),
            pltpu.VMEM((3, 2 * bins + 2 * HALO, 128), jnp.float32),
            pltpu.VMEM((3, 2, 32, 256), bf),
            pltpu.VMEM((bins + 2 * D2, 2, 32, 256), bf),
            pltpu.VMEM((3, 2 * bins + 2 * HALO, 128), jnp.float32),
            pltpu.SMEM((BAND + 1, n_blk), jnp.int32),
            pltpu.VMEM((bins // 2, 2 * bins, 128), jnp.float32),
            pltpu.VMEM((2 * bins, 128), bf),
            pltpu.SemaphoreType.DMA((5,)),
            pltpu.SemaphoreType.DMA((5,)),
            pltpu.SemaphoreType.DMA((5,)),
            pltpu.SemaphoreType.DMA((5,)),
            pltpu.SemaphoreType.DMA((5,)),
        ],
        compiler_params=pltpu.CompilerParams(
            collective_id=0, has_side_effects=True, vmem_limit_bytes=60 * 2**20
        ),
        name="contact",
    )(
        chrom_len,
        band_mask.T,
        features,
        conv_weight,
        conv_bias,
        proj_weight,
        proj_bias.reshape(1, -1),
        map_weight,
        map_bias.reshape(1, -1),
        head_weight.reshape(1, -1),
    )


def solution(mesh):
    return jax.shard_map(
        local,
        mesh=mesh,
        in_specs=(
            P(("dp", "blk"), "chan"),
            P("dp"),
            P("dp", None),
            P(None, None, None, "chan"),
            P(None, "chan"),
            P(),
            P(),
            P(None, None, "chan", None),
            P("chan"),
            P("chan"),
        ),
        out_specs=P(("dp", "blk"), "chan"),
        check_vma=False,
    )
```

```python
import jax
import jax.numpy as jnp
from jax import lax
from jax.experimental import pallas as pl
from jax.experimental.pallas import tpu as pltpu
from jax.sharding import PartitionSpec as P

F2 = 64
BAND = 3
D2 = 2
NEG = float("-inf")
HALO = 8
TILE_STEP = 4
SLOT = (1, 2, 0, 3)
NT = (((1,), (1,)), ((), ()))


PLAN = {
    -1: ((0, "last", 0), (1, "last", 0)),
    1: ((1, "both", 1), (0, "full", 2)),
    2: ((1, "full", 1), (0, "first", 3)),
    3: ((1, "full", 2),),
    4: ((1, "first", 3),),
}
ORDER = (4,3,2,-1,1)
SIZE = {"first": 8, "last": 8, "both": 16, "full": 64}


def kernel(
    n_blk,
    bins,
    len_ref,
    mask_hbm,
    x_hbm,
    cw_hbm,
    cb_hbm,
    pw_hbm,
    pb_hbm,
    mw_hbm,
    mb_hbm,
    hw_hbm,
    out_ref,
    feat,
    rim_out,
    rim_in,
    wts,
    cbias,
    pwt,
    pbias,
    mwt,
    small,
    mapt,
    mapw,
    pw4,
    pa_ref,
    pb_ref,
    pb4_ref,
    q_ref,
    gate_ref,
    gate4_ref,
    mask_ref,
    wide_ref,
    pbn_ref,
    send_sem,
    recv_sem,
    give_sem,
    pair_sem,
    loc_sem,
):
    dp = lax.axis_index("dp")
    blk = lax.axis_index("blk")
    chan = lax.axis_index("chan")
    other = 1 - chan
    half = x_hbm.shape[1]

    def dev(b, c):
        return (dp, b, c)

    barrier = pltpu.get_barrier_semaphore()

    def signal(b, c):
        pl.semaphore_signal(
            barrier, inc=1, device_id=dev(b, c), device_id_type=pl.DeviceIdType.MESH
        )

    for d in (4, 3, 2, -1, 1):
        inside = (blk + d >= 0) & (blk + d < n_blk)
        if d >= 3:
            inside = inside & (chan == 1)

        @pl.when(inside)
        def _(d=d):
            signal(blk + d, 0)
            signal(blk + d, 1)

    signal(blk, other)

    def joined(ref, sem):
        pltpu.make_async_copy(ref, ref, sem).wait()

    x_local = pltpu.make_async_copy(x_hbm, feat.at[chan, 0], loc_sem.at[0])
    mask_local = pltpu.make_async_copy(mask_hbm, mask_ref, loc_sem.at[1])
    pw_local = pltpu.make_async_copy(pw_hbm, pwt, loc_sem.at[2])
    pb_local = pltpu.make_async_copy(pb_hbm, pbias, loc_sem.at[3])
    for copy in (x_local, mask_local, pw_local, pb_local):
        copy.start()
    for src, dst, slot in (
        (mw_hbm, mwt.at[chan], 0),
        (mb_hbm, small.at[0, chan], 1),
        (hw_hbm, small.at[1, chan], 1),
        (cb_hbm, cbias.at[chan], 2),
        (cw_hbm, wts.at[chan], 3),
    ):
        pltpu.make_async_copy(src, dst, pair_sem.at[slot]).start()

    x_local.wait()
    for side in range(2):
        edge = feat[chan, 0, 0:16] if side == 0 else feat[chan, 0, bins - 16 : bins]
        edge = edge.astype(jnp.float32)[8 * side : 8 * side + 8]
        rim_out[side] = jnp.concatenate([edge[:, :128], edge[:, 128:]], axis=0).astype(
            jnp.bfloat16
        )

    def has(d):
        return jnp.where((blk - d >= 0) & (blk - d < n_blk), 1, 0)

    pl.semaphore_wait(barrier, 1 + 2 * has(-1) + 2 * has(1) + 2 * has(2) + has(3) + has(4))

    def feature_copy(d, n, sender):
        rc, kind, slot = PLAN[d][n]
        if kind == "full":
            src, dst = feat.at[sender, 0], feat.at[sender, slot]
        elif kind == "both":
            src, dst = rim_out, rim_in.at[sender, pl.ds(slot, 2)]
        else:
            src, dst = rim_out.at[0 if kind == "first" else 1], rim_in.at[sender, slot]
        return pltpu.make_async_remote_copy(
            src_ref=src,
            dst_ref=dst,
            send_sem=send_sem.at[min(max(d, 0), 1)],
            recv_sem=recv_sem.at[min(max(d, 0), 1)],
            device_id=dev(blk - d, rc),
            device_id_type=pl.DeviceIdType.MESH,
        )

    for d in ORDER:

        @pl.when((blk - d >= 0) & (blk - d < n_blk))
        def _(d=d):
            for n in range(len(PLAN[d])):
                feature_copy(d, n, chan).start()

    for src, dst, send, recv in (
        (mw_hbm, mwt.at[chan], give_sem.at[0], pair_sem.at[0]),
        (mb_hbm, small.at[0, chan], give_sem.at[1], pair_sem.at[1]),
        (hw_hbm, small.at[1, chan], give_sem.at[1], pair_sem.at[1]),
        (cb_hbm, cbias.at[chan], give_sem.at[2], pair_sem.at[2]),
        (x_hbm, feat.at[chan, 0], give_sem.at[3], loc_sem.at[4]),
        (cw_hbm.at[0], wts.at[chan, 0], give_sem.at[3], pair_sem.at[3]),
        (cw_hbm.at[1], wts.at[chan, 1], give_sem.at[3], pair_sem.at[3]),
    ):
        pltpu.make_async_remote_copy(
            src_ref=src,
            dst_ref=dst,
            send_sem=send,
            recv_sem=recv,
            device_id=dev(blk, other),
            device_id_type=pl.DeviceIdType.MESH,
        ).start()

    mapt[...] = jnp.zeros_like(mapt)
    joined(mwt, pair_sem.at[0])
    joined(small, pair_sem.at[1])
    joined(cbias, pair_sem.at[2])
    ho = mw_hbm.shape[2]
    for side in range(2):
        for s in range(3):
            for t in range(3):
                block = mwt[side, s, t]
                for k1 in range(2):
                    for k2 in range(2):
                        r0 = (2 * k2 + k1) * F2 + side * ho
                        c0 = (s + k1) * 256 + SLOT.index(t + k2) * F2
                        mapt[r0 : r0 + ho, c0 : c0 + F2] = block
    mapw[...] = jnp.transpose(mapt[...])
    pw_local.wait()
    pb_local.wait()
    for part in range(2):
        block = pwt[:, part * F2 : (part + 1) * F2]
        for twice in range(2):
            at = (2 * part + twice) * F2
            pw4[:, at : at + F2] = block
    proj_b = pbias[...].astype(jnp.float32)
    proj_b = jnp.concatenate(
        [proj_b[:, :F2], proj_b[:, :F2], proj_b[:, F2:], proj_b[:, F2:]], axis=1
    )
    sel_row = lax.broadcasted_iota(jnp.int32, (ho, 512), 0)
    sel_lane = lax.broadcasted_iota(jnp.int32, (ho, 512), 1) % F2
    bias_row = jnp.zeros((1, 512), jnp.float32)
    head_row = jnp.zeros((1, 512), jnp.float32)
    for side in range(2):
        spread = jnp.where(sel_lane == sel_row + side * ho, 1.0, 0.0).astype(jnp.bfloat16)
        bias_row += jnp.dot(small[0, side], spread, preferred_element_type=jnp.float32)
        head_row += jnp.dot(small[1, side], spread, preferred_element_type=jnp.float32)
    bias_map = bias_row[:, :128]
    h_row = lax.broadcasted_iota(jnp.int32, (8, 512), 0)
    h_lane = lax.broadcasted_iota(jnp.int32, (8, 512), 1) // F2
    h_want = (h_lane // 4) * 4 + (h_lane // 2) % 2 + 2 * (h_lane % 2)
    head_mat = jnp.where(
        h_row == h_want, jnp.broadcast_to(head_row, (8, 512)), 0.0
    ).astype(jnp.bfloat16)
    mask_local.wait()

    seg_a = bins + 2 * HALO
    seg_b = 2 * bins + 2 * HALO
    rows = seg_a + seg_b
    sub_b = lax.broadcasted_iota(jnp.int32, (seg_b, 128), 0)
    col_block = (chan * 2 * bins - HALO + bins + sub_b) // bins - 1

    def live_cols(block_shift, col_blk):
        at = blk + block_shift
        inside = (at >= 0) & (at < n_blk)
        at = lax.rem(at + n_blk, n_blk)
        live = jnp.zeros(col_blk.shape, jnp.int32)
        for o in range(BAND + 1):
            flag = jnp.where(inside, mask_ref[o, at], 0)
            live = jnp.where(col_blk - block_shift == o, flag, live)
        return live

    for v in range(3):
        gate_ref[v] = jnp.where(live_cols(v - 1, col_block) > 0, 0.0, NEG)

    n_tile = 2 * bins // 64
    low_lane = lax.broadcasted_iota(jnp.int32, (16, 128), 1) < F2

    def spread_cols(ref):
        for t in range(n_tile):
            for p in range(2):
                taps = [
                    ref[pl.ds(HALO + 64 * t + p + (SLOT[k] - 1) * D2, 16, stride=4), :]
                    for k in range(4)
                ]
                for k in range(2):
                    both = jnp.where(low_lane, taps[2 * k], taps[2 * k + 1])
                    place = (t, slice(16 * p, 16 * p + 16), slice(128 * k, 128 * k + 128))
                    yield place, both.astype(jnp.bfloat16)

    for v in range(3):
        for place, value in spread_cols(gate_ref.at[v]):
            gate4_ref[(v,) + place] = value

    feature_len = len_ref[0]
    total = n_blk * bins
    def received(entries, copies, sem):
        total = copies * sum(SIZE[kind] for _, kind, _ in entries)
        split = next(n for n in range(1, 33) if total % (8 * n) == 0 and total // n <= 128)
        joined(wide_ref.at[0:split, 0 : total // split], sem)

    def upto(k, rc=None):
        entries = [entry for d in range(1, k + 1) for entry in PLAN[d]]
        return [entry for entry in entries if rc is None or entry[0] == rc]

    below = jnp.minimum(blk, BAND + 1)
    above = jnp.minimum(n_blk - 1 - blk, BAND + 1)

    joined(mwt.at[0], give_sem.at[0])
    joined(small.at[:, 0], give_sem.at[1])
    joined(cbias.at[0], give_sem.at[2])
    blocks = 1 + 6 * cw_hbm.shape[2] // bins
    joined(q_ref.at[0:blocks], give_sem.at[3])
    @pl.when(above > 0)
    def _():
        received(PLAN[-1], 1, send_sem.at[0])

    for k in range(1, BAND + 2):

        @pl.when(below == k)
        def _(k=k):
            received(upto(k), 1, send_sem.at[1])

    joined(feat.at[0, 0], loc_sem.at[4])
    @pl.when(below > 0)
    def _():
        received(PLAN[-1][:1], 2, recv_sem.at[0])

    for k in range(1, BAND + 2):
        for rc in range(2):
            if rc == 0 and k > 2:
                continue

            @pl.when((jnp.where(chan == 0, jnp.minimum(above, 2), above) == k) & (chan == rc))
            def _(k=k, rc=rc):
                received(upto(k, rc), 2, recv_sem.at[1])

    joined(wts, pair_sem.at[3])


    def keep(mask, value):
        return jnp.concatenate(
            [
                jnp.where(mask, value[:, at : at + 128], 0.0)
                for at in range(0, value.shape[1], 128)
            ],
            axis=1,
        )

    def trunk(parts, first_rows):
        x = jnp.concatenate(
            [
                jnp.concatenate(
                    [
                        (
                            feat[side, k].astype(jnp.float32)
                            if kind == "block"
                            else jnp.concatenate(
                                [
                                    rim_in[side, k, 0:16].astype(jnp.float32)[:8],
                                    rim_in[side, k, 0:16].astype(jnp.float32)[8:],
                                ],
                                axis=1,
                            )
                        )
                        for kind, k in parts
                    ],
                    axis=0,
                )
                for side in range(2)
            ],
            axis=1,
        )
        rows = x.shape[0]
        r = lax.broadcasted_iota(jnp.int32, (rows, 128), 0)
        shift = jnp.where(r < first_rows, 0, chan * 2 * bins - first_rows)
        bin_p = blk * bins - HALO + r + shift
        ok_p = (bin_p >= 0) & (bin_p < feature_len)
        in_p = (bin_p >= 0) & (bin_p < total)

        def layer(h, level):
            e = 2 ** (level + 1)
            taps = [
                pltpu.roll(h, e, 0).astype(jnp.bfloat16),
                h.astype(jnp.bfloat16),
                pltpu.roll(h, rows - e, 0).astype(jnp.bfloat16),
            ]
            parts = []
            for side in range(2):
                acc = jnp.dot(taps[0], wts[side, level, 0], preferred_element_type=jnp.float32)
                for t in (1, 2):
                    acc += jnp.dot(taps[t], wts[side, level, t], preferred_element_type=jnp.float32)
                bias = cbias[side, level : level + 1].astype(jnp.float32)
                parts.append(jax.nn.relu(acc + bias))
            return (h + jnp.concatenate(parts, axis=1)).astype(jnp.bfloat16).astype(jnp.float32)

        h = layer(keep(ok_p, x), 0)
        h = layer(keep(in_p, h), 1)
        proj = (
            (jnp.dot(h.astype(jnp.bfloat16), pw4[...], preferred_element_type=jnp.float32) + proj_b)
            .astype(jnp.bfloat16)
            .astype(jnp.float32)
        )
        pa_ref[...] = jnp.where(ok_p[:seg_a], proj[:seg_a, :128], NEG)
        pb_ref[...] = jnp.where(ok_p[first_rows:], proj[first_rows:, 128:], NEG)

    @pl.when(chan == 0)
    def _():
        trunk([("rim", 0), ("block", 0), ("block", 2), ("rim", 3)], 0)

    @pl.when(chan == 1)
    def _():
        own = [("rim", 0), ("block", 0), ("rim", 1)]
        trunk(own + [("rim", 2), ("block", 1), ("block", 2), ("rim", 3)], seg_a)

    cols = 2 * bins
    for place, value in spread_cols(pb_ref):
        for v in range(3):
            pb4_ref[(v,) + place] = value + gate4_ref[(v,) + place]

    def build(r, t):
        v = 0 if r < D2 else (2 if r >= bins + D2 else 1)
        at = r + HALO - D2
        row = jnp.broadcast_to(pa_ref[at : at + 1, :], (16, 128)).astype(jnp.bfloat16)
        row = jnp.concatenate([jnp.concatenate([row, row], axis=1)] * 2, axis=0)
        q_ref[r, t] = jnp.maximum(pb4_ref[v, t] + row, jnp.bfloat16(0))

    out_row = lax.broadcasted_iota(jnp.int32, (8, cols), 0)
    out_lane = lax.broadcasted_iota(jnp.int32, (8, cols), 1) + chan * cols
    live_row = live_cols(0, out_lane // bins)
    live_row = jnp.where(blk * bins + out_lane < feature_len, live_row, 0)

    pbn_ref[...] = (pb_ref[HALO : HALO + cols] + gate_ref[1, HALO : HALO + cols]).astype(
        jnp.bfloat16
    )
    low_row = lax.broadcasted_iota(jnp.int32, (1, 128), 1) < F2
    bases = (0, 1, 4, 5)

    def conv(first):
        windows = jnp.concatenate(
            [
                jnp.concatenate([q_ref[8 * g + a + 2 * j, t] for j in range(4)], axis=1)
                for g in range(first, first + TILE_STEP)
                for t in range(n_tile)
                for a in bases
            ],
            axis=0,
        )
        wide = jnp.dot(windows, mapw[...], preferred_element_type=jnp.float32)
        at = 0
        for g in range(first, first + TILE_STEP):
            for t in range(n_tile):
                for j in range(4):
                    for p in range(2):
                        for k in range(2):
                            wide_ref[4 * g + j, pl.ds(64 * t + p + 2 * k, 16, stride=4), :] = wide[
                                at : at + 16, 128 * k : 128 * k + 128
                            ]
                        at += 16

    def finish(first):
        for g in range(first, first + TILE_STEP):
            sides = []
            for j, a in enumerate(bases):
                acc = jax.nn.relu(wide_ref[4 * g + j] + bias_map).astype(jnp.bfloat16)
                at = 8 * g + a + HALO
                row = jnp.where(low_row, pa_ref[at : at + 1, :], pa_ref[at + D2 : at + D2 + 1, :])
                row = jnp.broadcast_to(row, (16, 128)).astype(jnp.bfloat16)
                row = jnp.concatenate([row] * (cols // 16), axis=0)
                sides.append(acc + jnp.maximum(pbn_ref[...] + row, jnp.bfloat16(0)))
            mixed = jnp.concatenate(sides, axis=1)
            result = lax.dot_general(head_mat, mixed, NT, preferred_element_type=jnp.float32)
            live = jnp.where(blk * bins + 8 * g + out_row < feature_len, live_row, 0)
            out_ref[8 * g : 8 * g + 8, :] = jnp.where(live > 0, result, 0.0)

    done = 0
    for first in range(0, bins // 8, TILE_STEP):
        upto = 8 * (first + TILE_STEP) + 2 * D2
        for r in range(done, upto):
            for t in range(n_tile):
                build(r, t)
        done = upto
        conv(first)
        if first > 0:
            finish(first - TILE_STEP)
    finish(bins // 8 - TILE_STEP)


def local(
    features,
    chrom_len,
    band_mask,
    conv_weight,
    conv_bias,
    proj_weight,
    proj_bias,
    map_weight,
    map_bias,
    head_weight,
):
    import functools

    bins, half = features.shape
    n_blk = lax.axis_size("blk")
    bf = jnp.bfloat16
    any_spec = pl.BlockSpec(memory_space=pltpu.HBM)
    smem = pl.BlockSpec(memory_space=pltpu.SMEM)
    ho = map_weight.shape[2]
    return pl.pallas_call(
        functools.partial(kernel, n_blk, bins),
        out_shape=pltpu.VMEM((bins, 2 * bins), jnp.float32),
        in_specs=[smem] + [any_spec] * 9,
        out_specs=pl.BlockSpec(memory_space=pltpu.VMEM),
        scratch_shapes=[
            pltpu.VMEM((2, 3, bins, half), bf),
            pltpu.VMEM((2, 16, half // 2), bf),
            pltpu.VMEM((2, 4, 16, half // 2), bf),
            pltpu.VMEM((2,) + conv_weight.shape, bf),
            pltpu.VMEM((2,) + conv_bias.shape, bf),
            pltpu.VMEM(proj_weight.shape, bf),
            pltpu.VMEM((1, 2 * F2), bf),
            pltpu.VMEM((2,) + map_weight.shape, bf),
            pltpu.VMEM((2, 2, 1, ho), bf),
            pltpu.VMEM((256, 1024), bf),
            pltpu.VMEM((1024, 256), bf),
            pltpu.VMEM((proj_weight.shape[0], 256), bf),
            pltpu.VMEM((bins + 2 * HALO, 128), jnp.float32),
            pltpu.VMEM((2 * bins + 2 * HALO, 128), jnp.float32),
            pltpu.VMEM((3, 2, 32, 256), bf),
            pltpu.VMEM((bins + 2 * D2, 2, 32, 256), bf),
            pltpu.VMEM((3, 2 * bins + 2 * HALO, 128), jnp.float32),
            pltpu.VMEM((3, 2, 32, 256), bf),
            pltpu.SMEM((BAND + 1, n_blk), jnp.int32),
            pltpu.VMEM((bins // 2, 2 * bins, 128), jnp.float32),
            pltpu.VMEM((2 * bins, 128), bf),
            pltpu.SemaphoreType.DMA((2,)),
            pltpu.SemaphoreType.DMA((2,)),
            pltpu.SemaphoreType.DMA((4,)),
            pltpu.SemaphoreType.DMA((4,)),
            pltpu.SemaphoreType.DMA((5,)),
        ],
        compiler_params=pltpu.CompilerParams(
            collective_id=0, has_side_effects=True, vmem_limit_bytes=60 * 2**20
        ),
        name="contact",
    )(
        chrom_len,
        band_mask.T,
        features,
        conv_weight,
        conv_bias,
        proj_weight,
        proj_bias.reshape(1, -1),
        map_weight,
        map_bias.reshape(1, -1),
        head_weight.reshape(1, -1),
    )


def solution(mesh):
    return jax.shard_map(
        local,
        mesh=mesh,
        in_specs=(
            P(("dp", "blk"), "chan"),
            P("dp"),
            P("dp", None),
            P(None, None, None, "chan"),
            P(None, "chan"),
            P(),
            P(),
            P(None, None, "chan", None),
            P("chan"),
            P("chan"),
        ),
        out_specs=P(("dp", "blk"), "chan"),
        check_vma=False,
    )
```

```python
import jax
import jax.numpy as jnp
from jax import lax
from jax.experimental import pallas as pl
from jax.experimental.pallas import tpu as pltpu
from jax.sharding import PartitionSpec as P

F2 = 64
BAND = 3
D2 = 2
NEG = float("-inf")
HALO = 8
TILE_STEP = 4
SLOT = (1, 2, 0, 3)
NT = (((1,), (1,)), ((), ()))


PLAN = {
    -1: ((0, "last", 0), (1, "last", 0)),
    1: ((1, "both", 1), (0, "full", 2)),
    2: ((1, "full", 1), (0, "first", 3)),
    3: ((1, "full", 2),),
    4: ((1, "first", 3),),
}
ORDER = (4,3,2,-1,1)
RELAY = 2
STRAIGHT = 1
SIZE = {"first": 8, "last": 8, "both": 16, "full": 64}


def kernel(
    n_blk,
    bins,
    len_ref,
    mask_hbm,
    x_hbm,
    cw_hbm,
    cb_hbm,
    pw_hbm,
    pb_hbm,
    mw_hbm,
    mb_hbm,
    hw_hbm,
    out_ref,
    feat,
    rim_out,
    rim_in,
    wts,
    cbias,
    pwt,
    pbias,
    mwt,
    small,
    mapt,
    mapw,
    pw4,
    pa_ref,
    pb_ref,
    pb4_ref,
    q_ref,
    gate_ref,
    gate4_ref,
    mask_ref,
    wide_ref,
    pbn_ref,
    send_sem,
    recv_sem,
    give_sem,
    pair_sem,
    loc_sem,
    relay,
    relay_sem,
):
    dp = lax.axis_index("dp")
    blk = lax.axis_index("blk")
    chan = lax.axis_index("chan")
    other = 1 - chan
    half = x_hbm.shape[1]

    def dev(b, c):
        return (dp, b, c)

    barrier = pltpu.get_barrier_semaphore()

    def signal(b, c):
        pl.semaphore_signal(
            barrier, inc=1, device_id=dev(b, c), device_id_type=pl.DeviceIdType.MESH
        )

    for d in (4, 3, 2, -1, 1):
        inside = (blk + d >= 0) & (blk + d < n_blk)
        if d >= 3:
            inside = inside & (chan == 1)

        @pl.when(inside)
        def _(d=d):
            signal(blk + d, 0)
            signal(blk + d, 1)

    signal(blk, other)

    def joined(ref, sem):
        pltpu.make_async_copy(ref, ref, sem).wait()

    x_local = pltpu.make_async_copy(x_hbm, feat.at[chan, 0], loc_sem.at[0])
    mask_local = pltpu.make_async_copy(mask_hbm, mask_ref, loc_sem.at[1])
    pw_local = pltpu.make_async_copy(pw_hbm, pwt, loc_sem.at[2])
    pb_local = pltpu.make_async_copy(pb_hbm, pbias, loc_sem.at[3])
    for copy in (x_local, mask_local, pw_local, pb_local):
        copy.start()
    for src, dst, slot in (
        (mw_hbm, mwt.at[chan], 0),
        (mb_hbm, small.at[0, chan], 1),
        (hw_hbm, small.at[1, chan], 1),
        (cb_hbm, cbias.at[chan], 2),
        (cw_hbm, wts.at[chan], 3),
    ):
        pltpu.make_async_copy(src, dst, pair_sem.at[slot]).start()

    x_local.wait()
    for side in range(2):
        edge = feat[chan, 0, 0:16] if side == 0 else feat[chan, 0, bins - 16 : bins]
        edge = edge.astype(jnp.float32)[8 * side : 8 * side + 8]
        rim_out[side] = jnp.concatenate([edge[:, :128], edge[:, 128:]], axis=0).astype(
            jnp.bfloat16
        )

    def has(d):
        return jnp.where((blk - d >= 0) & (blk - d < n_blk), 1, 0)

    pl.semaphore_wait(barrier, 1 + 2 * has(-1) + 2 * has(1) + 2 * has(2) + has(3) + has(4))

    def feature_copy(d, n, sender):
        rc, kind, slot = PLAN[d][n]
        if kind == "full":
            src, dst = feat.at[sender, 0], feat.at[sender, slot]
        elif kind == "both":
            src, dst = rim_out, rim_in.at[sender, pl.ds(slot, 2)]
        else:
            src, dst = rim_out.at[0 if kind == "first" else 1], rim_in.at[sender, slot]
        return pltpu.make_async_remote_copy(
            src_ref=src,
            dst_ref=dst,
            send_sem=send_sem.at[min(max(d, 0), 1)],
            recv_sem=recv_sem.at[min(max(d, 0), 1)],
            device_id=dev(blk - d, rc),
            device_id_type=pl.DeviceIdType.MESH,
        )

    relayed = n_blk % 2 == 0
    pieces = [pl.ds(n * bins // RELAY, bins // RELAY) for n in range(RELAY)]

    def to_relay(n):
        return pltpu.make_async_remote_copy(
            src_ref=feat.at[chan, 0, pieces[n]],
            dst_ref=relay.at[pieces[n]],
            send_sem=send_sem.at[1],
            recv_sem=relay_sem.at[n],
            device_id=dev(blk + 1, chan),
            device_id_type=pl.DeviceIdType.MESH,
        )

    def from_relay(n):
        return pltpu.make_async_remote_copy(
            src_ref=relay.at[pieces[n]],
            dst_ref=feat.at[chan, 2, pieces[n]],
            send_sem=relay_sem.at[RELAY],
            recv_sem=recv_sem.at[1],
            device_id=dev(blk - 2, 0),
            device_id_type=pl.DeviceIdType.MESH,
        )

    first = pl.ds(0, STRAIGHT * bins // RELAY)
    straight = pltpu.make_async_remote_copy(
        src_ref=feat.at[chan, 0, first],
        dst_ref=feat.at[chan, 2, first],
        send_sem=send_sem.at[1],
        recv_sem=recv_sem.at[1],
        device_id=dev(blk - 1, 0),
        device_id_type=pl.DeviceIdType.MESH,
    )
    if relayed:

        @pl.when((blk % 2 == 0) & (blk > 0))
        def _():
            for n in range(STRAIGHT, RELAY):
                to_relay(n).start()

    for d in ORDER:

        @pl.when((blk - d >= 0) & (blk - d < n_blk))
        def _(d=d):
            for n, entry in enumerate(PLAN[d]):
                if relayed and d == 1 and entry[1] == "full":
                    pl.when(blk % 2 == 1)(feature_copy(d, n, chan).start)
                    pl.when(blk % 2 == 0)(straight.start)
                else:
                    feature_copy(d, n, chan).start()

    for src, dst, send, recv in (
        (mw_hbm, mwt.at[chan], give_sem.at[0], pair_sem.at[0]),
        (mb_hbm, small.at[0, chan], give_sem.at[1], pair_sem.at[1]),
        (hw_hbm, small.at[1, chan], give_sem.at[1], pair_sem.at[1]),
        (cb_hbm, cbias.at[chan], give_sem.at[2], pair_sem.at[2]),
        (x_hbm, feat.at[chan, 0], give_sem.at[3], loc_sem.at[4]),
        (cw_hbm.at[0], wts.at[chan, 0], give_sem.at[3], pair_sem.at[3]),
        (cw_hbm.at[1], wts.at[chan, 1], give_sem.at[3], pair_sem.at[3]),
    ):
        pltpu.make_async_remote_copy(
            src_ref=src,
            dst_ref=dst,
            send_sem=send,
            recv_sem=recv,
            device_id=dev(blk, other),
            device_id_type=pl.DeviceIdType.MESH,
        ).start()

    if relayed:

        @pl.when((blk % 2 == 1) & (blk > 1))
        def _():
            for n in range(STRAIGHT, RELAY):
                to_relay(n).wait_recv()
                from_relay(n).start()

    mapt[...] = jnp.zeros_like(mapt)
    joined(mwt, pair_sem.at[0])
    joined(small, pair_sem.at[1])
    joined(cbias, pair_sem.at[2])
    ho = mw_hbm.shape[2]
    for side in range(2):
        for s in range(3):
            for t in range(3):
                block = mwt[side, s, t]
                for k1 in range(2):
                    for k2 in range(2):
                        r0 = (2 * k2 + k1) * F2 + side * ho
                        c0 = (s + k1) * 256 + SLOT.index(t + k2) * F2
                        mapt[r0 : r0 + ho, c0 : c0 + F2] = block
    mapw[...] = jnp.transpose(mapt[...])
    pw_local.wait()
    pb_local.wait()
    for part in range(2):
        block = pwt[:, part * F2 : (part + 1) * F2]
        for twice in range(2):
            at = (2 * part + twice) * F2
            pw4[:, at : at + F2] = block
    proj_b = pbias[...].astype(jnp.float32)
    proj_b = jnp.concatenate(
        [proj_b[:, :F2], proj_b[:, :F2], proj_b[:, F2:], proj_b[:, F2:]], axis=1
    )
    sel_row = lax.broadcasted_iota(jnp.int32, (ho, 512), 0)
    sel_lane = lax.broadcasted_iota(jnp.int32, (ho, 512), 1) % F2
    bias_row = jnp.zeros((1, 512), jnp.float32)
    head_row = jnp.zeros((1, 512), jnp.float32)
    for side in range(2):
        spread = jnp.where(sel_lane == sel_row + side * ho, 1.0, 0.0).astype(jnp.bfloat16)
        bias_row += jnp.dot(small[0, side], spread, preferred_element_type=jnp.float32)
        head_row += jnp.dot(small[1, side], spread, preferred_element_type=jnp.float32)
    bias_map = bias_row[:, :128]
    h_row = lax.broadcasted_iota(jnp.int32, (8, 512), 0)
    h_lane = lax.broadcasted_iota(jnp.int32, (8, 512), 1) // F2
    h_want = (h_lane // 4) * 4 + (h_lane // 2) % 2 + 2 * (h_lane % 2)
    head_mat = jnp.where(
        h_row == h_want, jnp.broadcast_to(head_row, (8, 512)), 0.0
    ).astype(jnp.bfloat16)
    mask_local.wait()

    seg_a = bins + 2 * HALO
    seg_b = 2 * bins + 2 * HALO
    rows = seg_a + seg_b
    sub_b = lax.broadcasted_iota(jnp.int32, (seg_b, 128), 0)
    col_block = (chan * 2 * bins - HALO + bins + sub_b) // bins - 1

    def live_cols(block_shift, col_blk):
        at = blk + block_shift
        inside = (at >= 0) & (at < n_blk)
        at = lax.rem(at + n_blk, n_blk)
        live = jnp.zeros(col_blk.shape, jnp.int32)
        for o in range(BAND + 1):
            flag = jnp.where(inside, mask_ref[o, at], 0)
            live = jnp.where(col_blk - block_shift == o, flag, live)
        return live

    for v in range(3):
        gate_ref[v] = jnp.where(live_cols(v - 1, col_block) > 0, 0.0, NEG)

    n_tile = 2 * bins // 64
    low_lane = lax.broadcasted_iota(jnp.int32, (16, 128), 1) < F2

    def spread_cols(ref):
        for t in range(n_tile):
            for p in range(2):
                taps = [
                    ref[pl.ds(HALO + 64 * t + p + (SLOT[k] - 1) * D2, 16, stride=4), :]
                    for k in range(4)
                ]
                for k in range(2):
                    both = jnp.where(low_lane, taps[2 * k], taps[2 * k + 1])
                    place = (t, slice(16 * p, 16 * p + 16), slice(128 * k, 128 * k + 128))
                    yield place, both.astype(jnp.bfloat16)

    for v in range(3):
        for place, value in spread_cols(gate_ref.at[v]):
            gate4_ref[(v,) + place] = value

    feature_len = len_ref[0]
    total = n_blk * bins
    def received(entries, copies, sem):
        total = copies * sum(SIZE[kind] for _, kind, _ in entries)
        split = next(n for n in range(1, 33) if total % (8 * n) == 0 and total // n <= 128)
        joined(wide_ref.at[0:split, 0 : total // split], sem)

    def upto(k, rc=None):
        entries = [entry for d in range(1, k + 1) for entry in PLAN[d]]
        return [entry for entry in entries if rc is None or entry[0] == rc]

    below = jnp.minimum(blk, BAND + 1)
    above = jnp.minimum(n_blk - 1 - blk, BAND + 1)

    joined(mwt.at[0], give_sem.at[0])
    joined(small.at[:, 0], give_sem.at[1])
    joined(cbias.at[0], give_sem.at[2])
    blocks = 1 + 6 * cw_hbm.shape[2] // bins
    joined(q_ref.at[0:blocks], give_sem.at[3])
    @pl.when(above > 0)
    def _():
        received(PLAN[-1], 1, send_sem.at[0])

    for k in range(1, BAND + 2):

        @pl.when(below == k)
        def _(k=k):
            received(upto(k), 1, send_sem.at[1])

    if relayed:

        @pl.when((blk % 2 == 1) & (blk > 1))
        def _():
            joined(relay.at[STRAIGHT * bins // RELAY : bins], relay_sem.at[RELAY])

    joined(feat.at[0, 0], loc_sem.at[4])
    @pl.when(below > 0)
    def _():
        received(PLAN[-1][:1], 2, recv_sem.at[0])

    for k in range(1, BAND + 2):
        for rc in range(2):
            if rc == 0 and k > 2:
                continue

            @pl.when((jnp.where(chan == 0, jnp.minimum(above, 2), above) == k) & (chan == rc))
            def _(k=k, rc=rc):
                received(upto(k, rc), 2, recv_sem.at[1])

    joined(wts, pair_sem.at[3])


    def keep(mask, value):
        return jnp.concatenate(
            [
                jnp.where(mask, value[:, at : at + 128], 0.0)
                for at in range(0, value.shape[1], 128)
            ],
            axis=1,
        )

    def trunk(parts, first_rows):
        x = jnp.concatenate(
            [
                jnp.concatenate(
                    [
                        (
                            feat[side, k].astype(jnp.float32)
                            if kind == "block"
                            else jnp.concatenate(
                                [
                                    rim_in[side, k, 0:16].astype(jnp.float32)[:8],
                                    rim_in[side, k, 0:16].astype(jnp.float32)[8:],
                                ],
                                axis=1,
                            )
                        )
                        for kind, k in parts
                    ],
                    axis=0,
                )
                for side in range(2)
            ],
            axis=1,
        )
        rows = x.shape[0]
        r = lax.broadcasted_iota(jnp.int32, (rows, 128), 0)
        shift = jnp.where(r < first_rows, 0, chan * 2 * bins - first_rows)
        bin_p = blk * bins - HALO + r + shift
        ok_p = (bin_p >= 0) & (bin_p < feature_len)
        in_p = (bin_p >= 0) & (bin_p < total)

        def layer(h, level):
            e = 2 ** (level + 1)
            taps = [
                pltpu.roll(h, e, 0).astype(jnp.bfloat16),
                h.astype(jnp.bfloat16),
                pltpu.roll(h, rows - e, 0).astype(jnp.bfloat16),
            ]
            parts = []
            for side in range(2):
                acc = jnp.dot(taps[0], wts[side, level, 0], preferred_element_type=jnp.float32)
                for t in (1, 2):
                    acc += jnp.dot(taps[t], wts[side, level, t], preferred_element_type=jnp.float32)
                bias = cbias[side, level : level + 1].astype(jnp.float32)
                parts.append(jax.nn.relu(acc + bias))
            return (h + jnp.concatenate(parts, axis=1)).astype(jnp.bfloat16).astype(jnp.float32)

        h = layer(keep(ok_p, x), 0)
        h = layer(keep(in_p, h), 1)
        proj = (
            (jnp.dot(h.astype(jnp.bfloat16), pw4[...], preferred_element_type=jnp.float32) + proj_b)
            .astype(jnp.bfloat16)
            .astype(jnp.float32)
        )
        pa_ref[...] = jnp.where(ok_p[:seg_a], proj[:seg_a, :128], NEG)
        pb_ref[...] = jnp.where(ok_p[first_rows:], proj[first_rows:, 128:], NEG)

    @pl.when(chan == 0)
    def _():
        trunk([("rim", 0), ("block", 0), ("block", 2), ("rim", 3)], 0)

    @pl.when(chan == 1)
    def _():
        own = [("rim", 0), ("block", 0), ("rim", 1)]
        trunk(own + [("rim", 2), ("block", 1), ("block", 2), ("rim", 3)], seg_a)

    cols = 2 * bins
    for place, value in spread_cols(pb_ref):
        for v in range(3):
            pb4_ref[(v,) + place] = value + gate4_ref[(v,) + place]

    def build(r, t):
        v = 0 if r < D2 else (2 if r >= bins + D2 else 1)
        at = r + HALO - D2
        row = jnp.broadcast_to(pa_ref[at : at + 1, :], (16, 128)).astype(jnp.bfloat16)
        row = jnp.concatenate([jnp.concatenate([row, row], axis=1)] * 2, axis=0)
        q_ref[r, t] = jnp.maximum(pb4_ref[v, t] + row, jnp.bfloat16(0))

    out_row = lax.broadcasted_iota(jnp.int32, (8, cols), 0)
    out_lane = lax.broadcasted_iota(jnp.int32, (8, cols), 1) + chan * cols
    live_row = live_cols(0, out_lane // bins)
    live_row = jnp.where(blk * bins + out_lane < feature_len, live_row, 0)

    pbn_ref[...] = (pb_ref[HALO : HALO + cols] + gate_ref[1, HALO : HALO + cols]).astype(
        jnp.bfloat16
    )
    low_row = lax.broadcasted_iota(jnp.int32, (1, 128), 1) < F2
    bases = (0, 1, 4, 5)

    def conv(first):
        windows = jnp.concatenate(
            [
                jnp.concatenate([q_ref[8 * g + a + 2 * j, t] for j in range(4)], axis=1)
                for g in range(first, first + TILE_STEP)
                for t in range(n_tile)
                for a in bases
            ],
            axis=0,
        )
        wide = jnp.dot(windows, mapw[...], preferred_element_type=jnp.float32)
        at = 0
        for g in range(first, first + TILE_STEP):
            for t in range(n_tile):
                for j in range(4):
                    for p in range(2):
                        for k in range(2):
                            wide_ref[4 * g + j, pl.ds(64 * t + p + 2 * k, 16, stride=4), :] = wide[
                                at : at + 16, 128 * k : 128 * k + 128
                            ]
                        at += 16

    def finish(first):
        for g in range(first, first + TILE_STEP):
            sides = []
            for j, a in enumerate(bases):
                acc = jax.nn.relu(wide_ref[4 * g + j] + bias_map).astype(jnp.bfloat16)
                at = 8 * g + a + HALO
                row = jnp.where(low_row, pa_ref[at : at + 1, :], pa_ref[at + D2 : at + D2 + 1, :])
                row = jnp.broadcast_to(row, (16, 128)).astype(jnp.bfloat16)
                row = jnp.concatenate([row] * (cols // 16), axis=0)
                sides.append(acc + jnp.maximum(pbn_ref[...] + row, jnp.bfloat16(0)))
            mixed = jnp.concatenate(sides, axis=1)
            result = lax.dot_general(head_mat, mixed, NT, preferred_element_type=jnp.float32)
            live = jnp.where(blk * bins + 8 * g + out_row < feature_len, live_row, 0)
            out_ref[8 * g : 8 * g + 8, :] = jnp.where(live > 0, result, 0.0)

    done = 0
    for first in range(0, bins // 8, TILE_STEP):
        upto = 8 * (first + TILE_STEP) + 2 * D2
        for r in range(done, upto):
            for t in range(n_tile):
                build(r, t)
        done = upto
        conv(first)
        if first > 0:
            finish(first - TILE_STEP)
    finish(bins // 8 - TILE_STEP)


def local(
    features,
    chrom_len,
    band_mask,
    conv_weight,
    conv_bias,
    proj_weight,
    proj_bias,
    map_weight,
    map_bias,
    head_weight,
):
    import functools

    bins, half = features.shape
    n_blk = lax.axis_size("blk")
    bf = jnp.bfloat16
    any_spec = pl.BlockSpec(memory_space=pltpu.HBM)
    smem = pl.BlockSpec(memory_space=pltpu.SMEM)
    ho = map_weight.shape[2]
    return pl.pallas_call(
        functools.partial(kernel, n_blk, bins),
        out_shape=pltpu.VMEM((bins, 2 * bins), jnp.float32),
        in_specs=[smem] + [any_spec] * 9,
        out_specs=pl.BlockSpec(memory_space=pltpu.VMEM),
        scratch_shapes=[
            pltpu.VMEM((2, 3, bins, half), bf),
            pltpu.VMEM((2, 16, half // 2), bf),
            pltpu.VMEM((2, 4, 16, half // 2), bf),
            pltpu.VMEM((2,) + conv_weight.shape, bf),
            pltpu.VMEM((2,) + conv_bias.shape, bf),
            pltpu.VMEM(proj_weight.shape, bf),
            pltpu.VMEM((1, 2 * F2), bf),
            pltpu.VMEM((2,) + map_weight.shape, bf),
            pltpu.VMEM((2, 2, 1, ho), bf),
            pltpu.VMEM((256, 1024), bf),
            pltpu.VMEM((1024, 256), bf),
            pltpu.VMEM((proj_weight.shape[0], 256), bf),
            pltpu.VMEM((bins + 2 * HALO, 128), jnp.float32),
            pltpu.VMEM((2 * bins + 2 * HALO, 128), jnp.float32),
            pltpu.VMEM((3, 2, 32, 256), bf),
            pltpu.VMEM((bins + 2 * D2, 2, 32, 256), bf),
            pltpu.VMEM((3, 2 * bins + 2 * HALO, 128), jnp.float32),
            pltpu.VMEM((3, 2, 32, 256), bf),
            pltpu.SMEM((BAND + 1, n_blk), jnp.int32),
            pltpu.VMEM((bins // 2, 2 * bins, 128), jnp.float32),
            pltpu.VMEM((2 * bins, 128), bf),
            pltpu.SemaphoreType.DMA((2,)),
            pltpu.SemaphoreType.DMA((2,)),
            pltpu.SemaphoreType.DMA((4,)),
            pltpu.SemaphoreType.DMA((4,)),
            pltpu.SemaphoreType.DMA((5,)),
            pltpu.VMEM((bins, half), bf),
            pltpu.SemaphoreType.DMA((RELAY + 1,)),
        ],
        compiler_params=pltpu.CompilerParams(
            collective_id=0, has_side_effects=True, vmem_limit_bytes=60 * 2**20
        ),
        name="contact",
    )(
        chrom_len,
        band_mask.T,
        features,
        conv_weight,
        conv_bias,
        proj_weight,
        proj_bias.reshape(1, -1),
        map_weight,
        map_bias.reshape(1, -1),
        head_weight.reshape(1, -1),
    )


def solution(mesh):
    return jax.shard_map(
        local,
        mesh=mesh,
        in_specs=(
            P(("dp", "blk"), "chan"),
            P("dp"),
            P("dp", None),
            P(None, None, None, "chan"),
            P(None, "chan"),
            P(),
            P(),
            P(None, None, "chan", None),
            P("chan"),
            P("chan"),
        ),
        out_specs=P(("dp", "blk"), "chan"),
        check_vma=False,
    )
```
